512 devices in a mesh: row: 32 (over z_hi, x, core), col: 16 (over y, z_lo).
Axes of the slice: x: 4, y: 4, z: 16 (z_hi: 4, z_lo: 4; z = z_hi * 4 + z_lo), core: 2. Of those that a mesh axis runs over, the one named last changes fastest.
Arguments:
- queries: bfloat16 [4096, 2048], P('row', 'col'), may hold values from -48 to 48
- suffix_cache: bfloat16 [4096, 2048], P('row', 'col'), may hold values from -1.875 to 1.875
- suffix_leaf: int32 [32, 128], P('row'), may hold values from 0 to 31, never falling along the last dimension, each value on 1 to 8 neighbouring positions
- leaf_parent: int32 [32, 32], P('row'), may hold values from 0 to 31, as said below
- root_cache: bfloat16 [4096, 2048], P(('row', 'col')), may hold values from -2 to 2
- branch_cache: bfloat16 [32, 8192, 2048], P('row', 'col'), may hold values from -1.875 to 1.875
- branch_length: int32 [32], P('row'), may hold values from 1 to 8192, 196608 in all
- leaf_cache: bfloat16 [1024, 256, 2048], P('row', 'col'), may hold values from -1.875 to 1.875
- leaf_length: int32 [1024], P('row'), may hold values from 1 to 256, 131072 in all
Outputs:
- attention_out: bfloat16 [4096, 2048], P('row', 'col')
The draws below stay inside these ranges and needn't reach their ends.
Inputs may be any that keep to these rules, and one draw needn't show every extreme that they name: `suffix_leaf`: never falls along a row's tokens; each of the 32 leaves has 1 to 8 tokens. `leaf_parent`: in each row index every branch node is the parent of exactly 1 of its leaves, so at most 8 of that row's tokens lie under one branch node.
All inputs are finite; a program needn't handle non-finite values. No bound on the sum of `branch_length` or of `leaf_length` on one device may be relied on, other than what follows from the above.
Results may differ from the reference program's by a relative error of at most 0.0065.
Values may be sent and summed in bfloat16 or wider, within the bound.
No kernel may reach another device: no remote copies, remote signals or barrier semaphores. Data moves between devices by JAX's collectives and lax.ppermute only.
A program may use at most 64 MiB of HBM per device.

```python
import math
import jax
import jax.numpy as jnp
import numpy as np
from jax import lax

HEADS = 8
KV_HEADS = 4
HEAD_DIM = 256
TOK_ROW = 128
LEAF_ROW = 32
ROOT_LEN = 4096
BRANCH_LEN = 8192
LEAF_LEN = 256
QDIM = 2048
KVDIM = 2048
TOKENS = 4096
BRANCHES = 32
LEAVES = 1024
MOST = 8
CAP = 8
N_ROW = 32


def root_base(key):
    own_key = jax.random.fold_in(key, 7)
    values = 0.75 * jnp.clip(jax.random.normal(own_key, (ROOT_LEN, KVDIM), jnp.float32), -2.5, 2.5)
    return values


def root_drawn(key):
    values = root_base(key)
    return values


def draw_root_cache(key, part):
    return root_drawn(key).astype(jnp.bfloat16)


def draw_queries(key, part):
    own_key = jax.random.fold_in(key, 3)
    values = 3.4 * jnp.clip(jax.random.normal(own_key, (TOKENS, QDIM), jnp.float32), -6.0, 6.0)
    return values.astype(jnp.bfloat16)


def draw_leaf_parent(key, part):
    own_key = jax.random.fold_in(key, 5)
    row_keys = jax.random.split(own_key, BRANCHES)
    orders = jax.vmap(lambda row_key: jax.random.permutation(row_key, BRANCHES))(row_keys)
    columns = jnp.arange(LEAF_ROW) % BRANCHES
    return orders[:, columns].astype(jnp.int32)


def levels(rng, shape, cuts, low, top_value):
    def one(position, blocks):
        draws = jax.random.uniform(jax.random.fold_in(jax.random.fold_in(rng, 6), position), (blocks,), jnp.float32, low / len(cuts), top_value / len(cuts))
        return jnp.repeat(jnp.exp(draws), shape[position] // blocks).reshape((-1,) + (1,) * (len(shape) - position - 1))

    loudness = one(*cuts[0])
    for cut in cuts[1:]:
        loudness = loudness * one(*cut)
    return loudness


def split_up(amount, total, bound, lean):
    portions = [(1 << 20) // math.isqrt(standing ** lean) + 1 for standing in range(2, amount + 1)]
    spare, given = total - bound - (amount - 1), [1] * (amount - 1)
    while spare > 0:
        free = [i for i in range(amount - 1) if given[i] < bound]
        mass, remaining = sum([portions[i] for i in free]), spare
        for i in free:
            addition = min(bound - given[i], max(1, remaining * portions[i] // mass), spare)
            given[i] = given[i] + addition
            spare = spare - addition
    return np.array([bound] + given)


def ragged_sizes(key, number_of, total, bound, lean):
    if number_of == 2:
        one = jax.random.randint(key, (), max(1, total - bound), min(bound, total - 1) + 1)
        return jnp.stack([one, total - one])
    lengths = jnp.asarray(split_up(number_of, total, bound, lean), jnp.int32)
    pairs = (number_of - 1) // 2
    source_of, sink = lengths[1:1 + 2 * pairs:2], lengths[2:2 + 2 * pairs:2]
    margin = jnp.minimum(source_of - 1, bound - sink)
    moved = jax.random.randint(jax.random.fold_in(key, 1), (pairs,), 0, 1 << 20) % (margin + 1)
    lengths = lengths.at[1:1 + 2 * pairs:2].set(source_of - moved).at[2:2 + 2 * pairs:2].set(sink + moved)
    return lengths[jax.random.permutation(jax.random.fold_in(key, 2), number_of)]


def centred(stream_key, shape, deviation, most, pieces=(), kind=jnp.bfloat16):
    entries = deviation * jax.random.normal(stream_key, shape, jnp.float32)
    if pieces:
        entries = entries * levels(stream_key, shape, pieces, -0.22, 0.18)
    return jnp.clip(entries, -most, most).astype(kind)


def setup_inputs(seed: int = 0) -> dict:
    key_list = jax.random.split(jax.random.key(seed), 10)
    queries = draw_queries(jax.random.fold_in(key_list[9], 71), 0)
    suffix_cache = centred(key_list[1], (TOKENS, KVDIM), 0.75, 1.875, ((0, 32), (1, 16)))
    suffix_leaf = jax.vmap(lambda own: jnp.searchsorted(jnp.cumsum(ragged_sizes(own, LEAF_ROW, TOK_ROW, MOST, 2)), jnp.arange(TOK_ROW), side="right"))(jax.random.split(key_list[2], N_ROW)).reshape((N_ROW, TOK_ROW)).astype(jnp.int32)
    leaf_parent = draw_leaf_parent(jax.random.fold_in(key_list[9], 71), 0)
    root_cache = draw_root_cache(jax.random.fold_in(key_list[9], 71), 0)
    branch_cache = centred(key_list[5], (BRANCHES, BRANCH_LEN, KVDIM), 0.75, 1.875, ((0, 32), (1, 16)))
    branch_length = ragged_sizes(key_list[6], BRANCHES, 3 * BRANCHES * BRANCH_LEN // 4, BRANCH_LEN, 1).astype(jnp.int32)
    leaf_cache = centred(key_list[7], (LEAVES, LEAF_LEN, KVDIM), 0.75, 1.875, ((0, 32), (1, 16)))
    leaf_length = ragged_sizes(key_list[8], LEAVES, LEAVES * LEAF_LEN // 2, LEAF_LEN, 1).astype(jnp.int32)
    return {"queries": queries, "suffix_cache": suffix_cache, "suffix_leaf": suffix_leaf, "leaf_parent": leaf_parent, "root_cache": root_cache, "branch_cache": branch_cache, "branch_length": branch_length, "leaf_cache": leaf_cache, "leaf_length": leaf_length}


NEG = -1e+30

def finish(query_heads, key_heads, value_heads, scores, usable, row_count, equation):
    if usable is not None:
        key_mask = usable[:, None, None, :]
        scores = jnp.where(key_mask, scores, NEG)
    highest = lax.optimization_barrier(jnp.max(scores, axis=-1))
    weights = jnp.exp(scores - highest[..., None])
    if usable is not None:
        weights = jnp.where(key_mask, weights, 0.0)
    totals = lax.optimization_barrier(jnp.sum(weights, axis=-1))
    rounded = lax.optimization_barrier(weights.astype(jnp.bfloat16)).astype(jnp.float32)
    summed = jnp.einsum(equation, rounded, value_heads)
    return (highest.reshape(row_count, HEADS), totals.reshape(row_count, HEADS), summed.reshape(row_count, HEADS * HEAD_DIM))

def attend(queries, keys_values, usable):
    row_count = queries.shape[0]
    key_count = keys_values.shape[0]
    group_size = HEADS // KV_HEADS
    key_width = KV_HEADS * HEAD_DIM
    query_heads = queries.astype(jnp.float32).reshape(row_count, KV_HEADS, group_size, HEAD_DIM)
    key_heads = keys_values[:, :key_width].astype(jnp.float32).reshape(key_count, KV_HEADS, HEAD_DIM)
    value_heads = keys_values[:, key_width:].astype(jnp.float32).reshape(key_count, KV_HEADS, HEAD_DIM)
    scores = jnp.einsum('rgjd,kgd->rgjk', query_heads, key_heads) * (1.0 / math.sqrt(HEAD_DIM))
    return finish(query_heads, key_heads, value_heads, scores, usable, row_count, 'rgjk,kgd->rgjd')

def attend_each(queries, keys_values, usable):
    row_count = queries.shape[0]
    key_count = keys_values.shape[1]
    group_size = HEADS // KV_HEADS
    key_width = KV_HEADS * HEAD_DIM
    query_heads = queries.astype(jnp.float32).reshape(row_count, KV_HEADS, group_size, HEAD_DIM)
    key_heads = keys_values[:, :, :key_width].astype(jnp.float32).reshape(row_count, key_count, KV_HEADS, HEAD_DIM)
    value_heads = keys_values[:, :, key_width:].astype(jnp.float32).reshape(row_count, key_count, KV_HEADS, HEAD_DIM)
    scores = jnp.einsum('rgjd,rkgd->rgjk', query_heads, key_heads) * (1.0 / math.sqrt(HEAD_DIM))
    return finish(query_heads, key_heads, value_heads, scores, usable, row_count, 'rgjk,rkgd->rgjd')

def merge_state(earlier, others):
    highest = jnp.maximum(earlier[0], others[0])
    keep_first = jnp.exp(earlier[0] - highest)
    keep_second = jnp.exp(others[0] - highest)
    totals = earlier[1] * keep_first + others[1] * keep_second
    summed = earlier[2] * jnp.repeat(keep_first, HEAD_DIM, axis=1) + others[2] * jnp.repeat(keep_second, HEAD_DIM, axis=1)
    return (highest, totals, summed)

def reference(queries, suffix_cache, suffix_leaf, leaf_parent, root_cache, branch_cache, branch_length, leaf_cache, leaf_length):
    query_rows = queries.reshape(N_ROW, TOK_ROW, QDIM)
    suffix_rows = suffix_cache.reshape(N_ROW, TOK_ROW, KVDIM)
    row_ids = jnp.arange(N_ROW, dtype=jnp.int32)
    positions = jnp.arange(TOK_ROW, dtype=jnp.int32)
    leaf_places = jnp.arange(LEAF_LEN, dtype=jnp.int32)

    def row_local(inputs):
        row_queries, row_suffix, row_leaf, row_index = inputs
        running = attend(row_queries, root_cache, None)
        leaf_global = (row_index * LEAF_ROW + row_leaf).astype(jnp.int32)
        token_cache = leaf_cache[leaf_global]
        token_length = leaf_length[leaf_global]
        usable = leaf_places[None, :] < token_length[:, None]
        running = merge_state(running, attend_each(row_queries, token_cache, usable))
        usable = (row_leaf[:, None] == row_leaf[None, :]) & (positions[None, :] <= positions[:, None])
        running = merge_state(running, attend(row_queries, row_suffix, usable))
        return running
    local_state = lax.map(row_local, (query_rows, suffix_rows, suffix_leaf, row_ids))
    local_state = (local_state[0].reshape(TOKENS, HEADS), local_state[1].reshape(TOKENS, HEADS), local_state[2].reshape(TOKENS, QDIM))
    token_node = jnp.take_along_axis(leaf_parent, suffix_leaf, axis=1).astype(jnp.int32)
    node_hits = (token_node[:, :, None] == row_ids[None, None, :]).astype(jnp.int32)
    rank_in_node = lax.optimization_barrier(jnp.sum(node_hits * (jnp.cumsum(node_hits, axis=1) - 1), axis=2)).astype(jnp.int32)
    token_index = (row_ids[:, None] * TOK_ROW + positions[None, :]).astype(jnp.int32)
    slot_token = jnp.full((N_ROW, N_ROW, CAP), TOKENS, jnp.int32).at[token_node, row_ids[:, None], rank_in_node].set(token_index)
    padded = jnp.concatenate([queries, jnp.zeros((1, QDIM), queries.dtype)], axis=0)
    branch_places = jnp.arange(BRANCH_LEN, dtype=jnp.int32)

    def branch_part(inputs):
        node_slots, node_cache, node_length = inputs
        usable = (branch_places < node_length)[None, :]
        return attend(padded[node_slots.reshape(N_ROW * CAP)], node_cache, usable)
    branch_state = lax.map(branch_part, (slot_token, branch_cache, branch_length))
    flat_slot = (rank_in_node + row_ids[:, None] * CAP).astype(jnp.int32)
    picked = (branch_state[0][token_node, flat_slot].reshape(TOKENS, HEADS), branch_state[1][token_node, flat_slot].reshape(TOKENS, HEADS), branch_state[2][token_node, flat_slot].reshape(TOKENS, QDIM))
    highest, totals, summed = merge_state(local_state, picked)
    return (summed / jnp.repeat(totals, HEAD_DIM, axis=1)).astype(jnp.bfloat16)
```

```python
import jax
import jax.numpy as jnp
from jax import lax
from jax.experimental import pallas as pl
from jax.experimental.pallas import tpu as pltpu
from jax.sharding import Mesh, PartitionSpec as P

ROW = ("zh", "x", "core")
COL = ("y", "zl")
XC = ("x", "core")
XCZ = ("x", "core", "zl")
BF = jnp.bfloat16
F32 = jnp.float32
NEG = -1e30
FLOOR = -1e29
VMEM_LIMIT = 50 * 1024 * 1024


def iota(shape, dim):
    return lax.broadcasted_iota(jnp.int32, shape, dim)


def whole(shape):
    return pl.BlockSpec(shape, lambda: (0,) * len(shape))


SMEM = pl.BlockSpec(memory_space=pltpu.SMEM)
ANY = pl.BlockSpec(memory_space=pl.ANY)


def params():
    return pltpu.CompilerParams(vmem_limit_bytes=VMEM_LIMIT)


def slot_kernel(parent, leaf_ref, q_ref, root_ref, out_ref, slot_ref):
    leaf = leaf_ref[...]
    across = jnp.broadcast_to(leaf.astype(F32), (128, 128))
    down = across.T
    before = iota((128, 128), 0) < iota((128, 128), 1)
    rank = jnp.sum(jnp.where((across == down) & before, 1.0, 0.0), axis=0, keepdims=True)
    node = jnp.zeros((1, 128), jnp.int32)
    for leaf_id in range(32):
        node = jnp.where(leaf == leaf_id, parent[0, leaf_id], node)
    slot = node * 8 + rank.astype(jnp.int32)
    slot_ref[...] = slot
    pick = jnp.where(iota((256, 128), 0) == slot, 1.0, 0.0).astype(BF)
    routed = jnp.dot(pick, q_ref[...], preferred_element_type=F32).astype(BF)
    root = root_ref[...].astype(F32)
    blocks = jnp.concatenate([root[:, j * 128 : (j + 1) * 128] for j in range(16)], axis=0).astype(BF)
    for z in range(4):
        out_ref[z, 0:64] = routed[z * 64 : (z + 1) * 64]
        out_ref[z, 64:192] = blocks


def route_slots(parent, leaf, queries, root):
    return pl.pallas_call(
        slot_kernel,
        out_shape=(
            jax.ShapeDtypeStruct((4, 192, 128), BF),
            jax.ShapeDtypeStruct((1, 128), jnp.int32),
        ),
        in_specs=[SMEM, whole((1, 128)), whole((128, 128)), whole((8, 2048))],
        out_specs=(whole((4, 192, 128)), whole((1, 128))),
        compiler_params=params(),
        name="route_slots",
    )(parent, leaf, queries, root)


def pack_cache(where, cache, extra):
    rows = 2048 + (128 if extra is not None else 0)

    def kernel(where_ref, *refs):
        cache_ref = refs[0]
        outs = refs[-4:-1]
        sems = refs[-1]
        copies = []
        for s in range(3):
            target = (where_ref[0] + (s + 1)) & 3
            for part in range(4):
                start = (part // 2) * 1024 + (part % 2) * 128
                lane = pl.multiple_of(target * 256 + start, 128)
                copies.append(
                    pltpu.make_async_copy(
                        cache_ref.at[:, pl.ds(lane, 128)],
                        outs[s].at[pl.ds(part * 512, 512), :],
                        sems.at[s, part],
                    )
                )
            if extra is not None:
                copies.append(
                    pltpu.make_async_copy(refs[1], outs[s].at[pl.ds(2048, 128), :], sems.at[s, 4])
                )
        for copy in copies:
            copy.start()
        for copy in copies:
            copy.wait()

    operands = (where, cache) + ((extra,) if extra is not None else ())
    return pl.pallas_call(
        kernel,
        out_shape=tuple(jax.ShapeDtypeStruct((rows, 128), BF) for _ in range(3)),
        in_specs=[SMEM] + [ANY] * (len(operands) - 1),
        out_specs=(ANY, ANY, ANY),
        scratch_shapes=[pltpu.SemaphoreType.DMA((3, 5))],
        compiler_params=params(),
        name="pack_cache",
    )(*operands)


def softmax_parts(scores, values):
    highest = scores[0].max(axis=1, keepdims=True)
    for part in scores[1:]:
        highest = jnp.maximum(highest, part.max(axis=1, keepdims=True))
    highest = jnp.maximum(highest, FLOOR).astype(BF).astype(F32)
    total = 0.0
    summed = 0.0
    for part, value in zip(scores, values):
        weights = jnp.exp(part - highest)
        total = total + jnp.sum(weights, axis=1, keepdims=True)
        summed = summed + jnp.dot(weights.astype(BF), value, preferred_element_type=F32)
    return highest, total, summed


def score(queries, keys):
    return lax.dot_general(
        queries, keys, (((1,), (1,)), ((), ())), preferred_element_type=F32
    ) * (1.0 / 16.0)


def split_total(total):
    upper = total.astype(BF).astype(F32)
    return upper, total - upper


def lane_stats(highest, total, first):
    upper, lower = split_total(total)
    rows = highest.shape[0]
    lane = iota((rows, 128), 1)
    place = jnp.where(lane == first, highest, 0.0)
    place = jnp.where(lane == first + 1, upper, place)
    return jnp.where(lane == first + 2, lower, place)


def piece(ref, kv):
    base = kv * 1024
    return jnp.concatenate([ref[base : base + 512], ref[base + 512 : base + 1024]], axis=1)


def branch_kernel(info, q_ref, kown, vown, p1, p2, p3, out_ref):
    y = info[0]
    zl = info[1]
    length = info[2]
    loaded = q_ref[...].reshape(8, 4, 32, 128)
    blocks = [loaded[:, z].reshape(256, 128) for z in range(4)]
    keys = [kown[...]] + [piece(ref, 0) for ref in (p1, p2, p3)]
    values = [vown[...]] + [piece(ref, 1) for ref in (p1, p2, p3)]
    row16 = iota((256, 128), 0) & 31
    for h in range(2):
        queries = jnp.concatenate([blocks[2 * h], blocks[2 * h + 1]], axis=1)
        scores = []
        for s in range(4):
            source = (y - s) & 3
            place = (source * 4 + zl) * 512 + iota((256, 512), 1)
            scores.append(jnp.where(place < length, score(queries, keys[s]), NEG))
        highest, total, summed = softmax_parts(scores, values)
        first = jnp.where(row16 < 16, 0, 64)
        stats = lane_stats(highest, total, first)
        for xc in range(8):
            low = xc * 32
            packed = (stats[low : low + 16] + stats[low + 16 : low + 32]).astype(BF)
            for half in range(2):
                out_ref[xc * 4 + 2 * h + half, 0:32] = summed[
                    low : low + 32, half * 128 : (half + 1) * 128
                ].astype(BF)
                out_ref[xc * 4 + 2 * h + half, 32:48] = packed


def branch_attend(info, arrived, cache, pieces):
    head = pl.BlockSpec((512, 256), lambda i, info: (0, info[0]))
    head_value = pl.BlockSpec((512, 256), lambda i, info: (0, 4 + info[0]))
    full = lambda shape: pl.BlockSpec(shape, lambda i, info: (0,) * len(shape))
    rows = pieces[0].shape[0]
    return pl.pallas_call(
        branch_kernel,
        out_shape=jax.ShapeDtypeStruct((32, 48, 128), BF),
        grid_spec=pltpu.PrefetchScalarGridSpec(
            num_scalar_prefetch=1,
            grid=(1,),
            in_specs=[full((32, 32, 128)), head, head_value] + [full((rows, 128))] * 3,
            out_specs=full((32, 48, 128)),
        ),
        compiler_params=params(),
        name="branch_attend",
    )(info, arrived, cache, cache, *pieces)


def merge_kernel(in_ref, out_ref):
    loaded = in_ref[...].astype(F32).reshape(8, 4, 48, 128)
    data = [loaded[:, z, 0:32] for z in range(4)]
    stats = [loaded[:, z, 32:48] for z in range(4)]

    def column(stat, j):
        return jnp.concatenate([stat[:, :, j : j + 1], stat[:, :, 64 + j : 65 + j]], axis=1)

    peaks = [column(stat, 0) for stat in stats]
    highest = jnp.maximum(jnp.maximum(peaks[0], peaks[1]), jnp.maximum(peaks[2], peaks[3]))
    total = 0.0
    summed = 0.0
    for z in range(4):
        factor = jnp.exp(peaks[z] - highest)
        total = total + factor * (column(stats[z], 1) + column(stats[z], 2))
        summed = summed + factor * data[z]
    highest = highest.reshape(8, 4, 8, 1)
    total = total.reshape(8, 4, 8, 1)
    summed = summed.reshape(8, 4, 8, 128)
    first = (iota((64, 128), 0) >> 4) * 32
    for z in range(4):
        out_ref[z, 0:64] = summed[:, z].reshape(64, 128).astype(BF)
        placed = lane_stats(highest[:, z].reshape(64, 1), total[:, z].reshape(64, 1), first)
        out_ref[z, 64:80] = (
            placed[0:16] + placed[16:32] + placed[32:48] + placed[48:64]
        ).astype(BF)


def merge_node(partials):
    return pl.pallas_call(
        merge_kernel,
        out_shape=jax.ShapeDtypeStruct((4, 80, 128), BF),
        in_specs=[whole((32, 48, 128))],
        out_specs=whole((4, 80, 128)),
        compiler_params=params(),
        name="merge_node",
    )(partials)


def local_kernel(
    info, leaf_ref, lengths_ref, kown, vown, p1, p2, p3, root_ref, l0, l1, l2, l3,
    out0, out1, out2, out3, gathered, outgoing,
):
    y = info[0]
    zl = info[1]
    for s, ref in enumerate((l0, l1, l2, l3)):
        gathered[(zl - s) & 3] = ref[...]
    leaf_row = jnp.broadcast_to(leaf_ref[...].astype(F32), (128, 128))
    leaf_col = leaf_row.T
    first_half = (y & 1) * 2
    suffix_k = jnp.concatenate(
        [gathered[first_half, 128:256], gathered[first_half + 1, 128:256]], axis=1
    )
    suffix_v = jnp.concatenate(
        [gathered[first_half, 256:384], gathered[first_half + 1, 256:384]], axis=1
    )
    root = root_ref[...].reshape(8, 4, 4, 32, 128)
    root_parts = [root[:, :, j].reshape(1024, 128) for j in range(4)]
    root_k = jnp.concatenate(root_parts[0:2], axis=1)
    root_v = jnp.concatenate(root_parts[2:4], axis=1)
    leaf_keys = [kown[...]] + [piece(ref, 0) for ref in (p1, p2, p3)]
    leaf_values = [vown[...]] + [piece(ref, 1) for ref in (p1, p2, p3)]
    token = iota((128, 128), 0)
    key_token = iota((128, 128), 1)
    suffix_ok = (leaf_row == leaf_col) & (key_token <= token) & ((key_token & 3) == zl)
    key_slot = iota((1, 512), 1)
    first = (iota((128, 128), 0) >> 4) * 16
    for h in range(2):
        queries = jnp.concatenate([gathered[2 * h, 0:128], gathered[2 * h + 1, 0:128]], axis=1)
        scores = [score(queries, root_k)]
        for s in range(4):
            source = (y - s) & 3
            place = (source * 4 + zl) * 16 + (key_slot & 15)
            key_leaf = jnp.where(place < lengths_ref[...], key_slot >> 4, -1).astype(F32)
            scores.append(
                jnp.where(leaf_col[:, 0:1] == key_leaf, score(queries, leaf_keys[s]), NEG)
            )
        scores.append(jnp.where(suffix_ok, score(queries, suffix_k), NEG))
        highest, total, summed = softmax_parts(scores, [root_v] + leaf_values + [suffix_v])
        stats = lane_stats(highest, total, first)
        packed = stats[0:16]
        for g in range(1, 8):
            packed = packed + stats[g * 16 : (g + 1) * 16]
        for half in range(2):
            outgoing[2 * h + half, 0:128] = summed[:, half * 128 : (half + 1) * 128].astype(BF)
            outgoing[2 * h + half, 128:144] = packed.astype(BF)
    for s, ref in enumerate((out0, out1, out2, out3)):
        ref[...] = outgoing[(zl + s) & 3]


def local_attend(info, leaf, lengths, cache, pieces, root, gathered):
    head = pl.BlockSpec((512, 256), lambda i, info: (0, info[0]))
    head_value = pl.BlockSpec((512, 256), lambda i, info: (0, 4 + info[0]))
    full = lambda shape: pl.BlockSpec(shape, lambda i, info: (0,) * len(shape))
    return pl.pallas_call(
        local_kernel,
        out_shape=tuple(jax.ShapeDtypeStruct((144, 128), BF) for _ in range(4)),
        grid_spec=pltpu.PrefetchScalarGridSpec(
            num_scalar_prefetch=1,
            grid=(1,),
            in_specs=[full((1, 128)), full((1, 512)), head, head_value]
            + [full((2048, 128))] * 3
            + [full((8, 512, 128))]
            + [full((384, 128))] * 4,
            out_specs=tuple(full((144, 128)) for _ in range(4)),
            scratch_shapes=[pltpu.VMEM((4, 384, 128), BF), pltpu.VMEM((4, 144, 128), BF)],
        ),
        compiler_params=params(),
        name="local_attend",
    )(info, leaf, lengths, cache, cache, *pieces, root, *gathered)


def final_kernel(slot_ref, branch_ref, l0, l1, l2, l3, out_ref):
    pick = jnp.where(iota((256, 128), 0) == slot_ref[...], 1.0, 0.0).astype(BF)

    def to_tokens(values):
        return lax.dot_general(
            pick, values, (((0,), (0,)), ((), ())), preferred_element_type=F32
        )

    branch = branch_ref[...]
    branch_sum = to_tokens(branch[:, 0:64].reshape(256, 128))
    lane16 = iota((16, 128), 1) >> 5
    spread = []
    for z in range(4):
        stat = branch[z, 64:80].astype(F32)
        for g in range(4):
            spread.append(jnp.where(lane16 == g, stat, 0.0))
    branch_stat = to_tokens(jnp.concatenate(spread, axis=0).astype(BF))
    lane = iota((128, 128), 1)

    def lane_pick(values, hit):
        return jnp.sum(jnp.where(hit, values, 0.0), axis=1, keepdims=True)

    column = lane & 31
    peaks = [lane_pick(branch_stat, column == 0)]
    totals = [lane_pick(branch_stat, (column == 1) | (column == 2))]
    sums = [branch_sum]
    first = (iota((128, 128), 0) >> 4) * 16
    for ref in (l0, l1, l2, l3):
        sums.append(ref[0:128].astype(F32))
        stat = ref[128:144].astype(F32)
        stat = jnp.concatenate([stat] * 8, axis=0)
        peaks.append(lane_pick(stat, lane == first))
        totals.append(lane_pick(stat, (lane == first + 1) | (lane == first + 2)))
    highest = peaks[0]
    for peak in peaks[1:]:
        highest = jnp.maximum(highest, peak)
    total = 0.0
    summed = 0.0
    for peak, part, value in zip(peaks, totals, sums):
        factor = jnp.exp(peak - highest)
        total = total + factor * part
        summed = summed + factor * value
    out_ref[...] = (summed / total).astype(BF)


def finish(slot, branch, parts):
    return pl.pallas_call(
        final_kernel,
        out_shape=jax.ShapeDtypeStruct((128, 128), BF),
        in_specs=[whole((1, 128)), whole((4, 80, 128))] + [whole((144, 128))] * 4,
        out_specs=whole((128, 128)),
        compiler_params=params(),
        name="finish",
    )(slot, branch, *parts)


def shift(values, axis, step):
    return lax.ppermute(values, axis, [(i, (i + step) % 4) for i in range(4)])


def exchange(values, axis):
    return lax.all_to_all(values, axis, split_axis=0, concat_axis=0, tiled=True)


def on_device(
    queries, suffix_cache, suffix_leaf, leaf_parent, root_cache,
    branch_cache, branch_length, leaf_cache, leaf_length,
):
    y = lax.axis_index("y")
    zl = lax.axis_index("zl")
    info = jnp.stack([y, zl, branch_length[0]]).astype(jnp.int32)
    branch_rows = branch_cache.reshape(512, 2048)
    leaf_rows = leaf_cache.reshape(512, 2048)

    routed, slot = route_slots(leaf_parent, suffix_leaf, queries, root_cache)
    arrived = exchange(routed, "zh")

    branch_out = pack_cache(info, branch_rows, suffix_cache)
    branch_in = [shift(branch_out[s], "y", s + 1) for s in range(3)]
    leaf_out = pack_cache(info, leaf_rows, None)
    leaf_in = [shift(leaf_out[s], "y", s + 1) for s in range(3)]

    onward = arrived[:, 0:64].reshape(4, 8, 8, 128).transpose(1, 0, 2, 3).reshape(8, 1, 32, 128)
    onward = jnp.broadcast_to(onward, (8, 4, 32, 128)).reshape(32, 32, 128)
    node_queries = exchange(onward, XCZ)

    root = arrived[:, 64:192].reshape(4, 2, 4, 2, 8, 128).transpose(2, 1, 3, 0, 4, 5)
    root = root.reshape(4, 4 * 32, 128)
    root_parts = [lax.dynamic_index_in_dim(root, y, 0, keepdims=False)]
    for s in range(3):
        part = lax.dynamic_index_in_dim(root, (y + (s + 1)) & 3, 0, keepdims=False)
        root_parts.append(shift(part, "y", s + 1))
    root_all = lax.all_gather(jnp.concatenate(root_parts, axis=0), XC, axis=0, tiled=False)

    partials = branch_attend(info, node_queries, branch_rows, branch_in)

    blocks = [suffix_cache] + [part[2048:2176] for part in branch_in]

    def chosen(source):
        step = (y - source) & 3
        return lax.select_n(step, *blocks)

    mine = jnp.concatenate([queries, chosen(y // 2), chosen(2 + y // 2)], axis=0)
    gathered = [mine] + [shift(mine, "zl", s + 1) for s in range(3)]

    returned = exchange(partials, XCZ)
    merged = merge_node(returned)
    back = exchange(merged, "zh")

    lengths = jnp.repeat(leaf_length, 16).reshape(1, 512)
    local = local_attend(info, suffix_leaf, lengths, leaf_rows, leaf_in, root_all, gathered)
    parts = [local[0]] + [shift(local[s + 1], "zl", s + 1) for s in range(3)]
    return finish(slot, back, parts)


def solution(mesh):
    fine = Mesh(mesh.devices.reshape(4, 4, 2, 4, 4), ("zh", "x", "core", "y", "zl"))
    in_specs = (
        P(ROW, COL),
        P(ROW, COL),
        P(ROW, None),
        P(ROW, None),
        P(ROW + COL, None),
        P(ROW, COL, None),
        P(ROW),
        P(ROW, COL, None),
        P(ROW),
    )
    return jax.shard_map(
        on_device, mesh=fine, in_specs=in_specs, out_specs=P(ROW, COL), check_vma=False
    )
```

```python
import jax
import jax.numpy as jnp
from jax import lax
from jax.experimental import pallas as pl
from jax.experimental.pallas import tpu as pltpu
from jax.sharding import Mesh, PartitionSpec as P

ROW = ("zh", "x", "core")
COL = ("y", "zl")
XC = ("x", "core")
XCZ = ("x", "core", "zl")
BF = jnp.bfloat16
F32 = jnp.float32
NEG = -1e30
FLOOR = -1e29
COST_FLOPS = 30_000_000_000
VMEM_LIMIT = 50 * 1024 * 1024


def iota(shape, dim):
    return lax.broadcasted_iota(jnp.int32, shape, dim)


def whole(shape):
    return pl.BlockSpec(shape, lambda: (0,) * len(shape))


SMEM = pl.BlockSpec(memory_space=pltpu.SMEM)
HBM = pl.BlockSpec(memory_space=pltpu.HBM)


def params():
    return pltpu.CompilerParams(vmem_limit_bytes=VMEM_LIMIT)


def first_kernel(
    parent, leaf_hbm, q_hbm, root_hbm, cache_hbm, out_ref, slot_ref, sent_hbm,
    leaf_ref, q_ref, root_ref, split_ref, sems, bulk,
):
    copies = [
        pltpu.make_async_copy(source, target, sems.at[i])
        for i, (source, target) in enumerate(
            ((root_hbm, root_ref), (leaf_hbm, leaf_ref), (q_hbm, q_ref))
        )
    ]
    for copy in copies:
        copy.start()
    moves = []
    for target in range(4):
        for part in range(4):
            lane = (part // 2) * 1024 + target * 256 + (part % 2) * 128
            moves.append(
                pltpu.make_async_copy(
                    cache_hbm.at[:, pl.ds(lane, 128)],
                    sent_hbm.at[target, pl.ds(part * 512, 512), :],
                    bulk.at[target, part],
                )
            )
    for move in moves:
        move.start()
    for copy in copies:
        copy.wait()
    root = root_ref[...].astype(F32)
    splits = []
    for target in range(4):
        lanes = [kv * 1024 + target * 256 + half * 128 for kv in range(2) for half in range(2)]
        split_ref[target] = jnp.concatenate([root[:, l : l + 128] for l in lanes], axis=0).astype(BF)
        splits.append(
            pltpu.make_async_copy(
                split_ref.at[target], sent_hbm.at[target, pl.ds(2048, 32), :], sems.at[3 + target]
            )
        )
        splits[-1].start()
    leaf = leaf_ref[...]
    across = jnp.broadcast_to(leaf.astype(F32), (128, 128))
    down = across.T
    before = iota((128, 128), 0) < iota((128, 128), 1)
    rank = jnp.sum(jnp.where((across == down) & before, 1.0, 0.0), axis=0, keepdims=True)
    node = jnp.zeros((1, 128), jnp.int32)
    for leaf_id in range(32):
        node = jnp.where(leaf == leaf_id, parent[0, leaf_id], node)
    slot = node * 8 + rank.astype(jnp.int32)
    slot_ref[...] = slot
    pick = jnp.where(iota((256, 128), 0) == slot, 1.0, 0.0).astype(BF)
    routed = jnp.dot(pick, q_ref[...], preferred_element_type=F32).astype(BF)
    out_ref[...] = routed.reshape(4, 64, 128)
    for copy in moves + splits:
        copy.wait()


def first_stage(parent, leaf, queries, root, cache):
    return pl.pallas_call(
        first_kernel,
        out_shape=(
            jax.ShapeDtypeStruct((4, 64, 128), BF),
            jax.ShapeDtypeStruct((1, 128), jnp.int32),
            jax.ShapeDtypeStruct((4, 2080, 128), BF),
        ),
        in_specs=[SMEM, HBM, HBM, HBM, HBM],
        out_specs=(whole((4, 64, 128)), whole((1, 128)), HBM),
        scratch_shapes=[
            pltpu.VMEM((1, 128), jnp.int32),
            pltpu.VMEM((128, 128), BF),
            pltpu.VMEM((8, 2048), BF),
            pltpu.VMEM((4, 32, 128), BF),
            pltpu.SemaphoreType.DMA((7,)),
            pltpu.SemaphoreType.DMA((4, 4)),
        ],
        compiler_params=params(),
        name="first_stage",
    )(parent, leaf, queries, root, cache)


def pack_kernel(info, cache_hbm, g0, g1, g2, g3, out1, out2, out3, own, blocks, sems, bulk):
    y = info[0]
    zl = info[1]
    moves = []
    for s, out in enumerate((out1, out2, out3)):
        target = (y + (s + 1)) & 3
        for part in range(4):
            start = (part // 2) * 1024 + (part % 2) * 128
            lane = pl.multiple_of(target * 256 + start, 128)
            moves.append(
                pltpu.make_async_copy(
                    cache_hbm.at[:, pl.ds(lane, 128)],
                    out.at[pl.ds(part * 512, 512), :],
                    bulk.at[s, part],
                )
            )
    for move in moves:
        move.start()
    firsts = [
        pltpu.make_async_copy(ref.at[pl.ds(128, 128), :], blocks.at[(zl - s) & 3], sems.at[0, s])
        for s, ref in enumerate((g0, g1, g2, g3))
    ]
    for copy in firsts:
        copy.start()
    for copy in firsts:
        copy.wait()
    seconds = []
    for s, (out, row) in enumerate(((own, 0), (out1, 2048), (out2, 2048), (out3, 2048))):
        first = (((y + s) & 3) & 1) * 2
        for half in range(2):
            seconds.append(
                pltpu.make_async_copy(
                    blocks.at[first + half],
                    out.at[pl.ds(row + half * 128, 128), :],
                    sems.at[1 + half, s],
                )
            )
    for copy in seconds:
        copy.start()
    for copy in moves + seconds:
        copy.wait()


def pack_leaf(info, cache, gathered):
    return pl.pallas_call(
        pack_kernel,
        out_shape=tuple(jax.ShapeDtypeStruct((2304, 128), BF) for _ in range(3))
        + (jax.ShapeDtypeStruct((256, 128), BF),),
        in_specs=[SMEM] + [HBM] * 5,
        out_specs=(HBM, HBM, HBM, HBM),
        scratch_shapes=[
            pltpu.VMEM((4, 128, 128), BF),
            pltpu.SemaphoreType.DMA((3, 4)),
            pltpu.SemaphoreType.DMA((3, 4)),
        ],
        compiler_params=params(),
        name="pack_leaf",
    )(info, cache, *gathered)


def softmax_parts(scores, values):
    highest = scores[0].max(axis=1, keepdims=True)
    for part in scores[1:]:
        highest = jnp.maximum(highest, part.max(axis=1, keepdims=True))
    highest = jnp.maximum(highest, FLOOR).astype(BF).astype(F32)
    total = 0.0
    summed = 0.0
    for part, value in zip(scores, values):
        weights = jnp.exp(part - highest)
        total = total + jnp.sum(weights, axis=1, keepdims=True)
        summed = summed + jnp.dot(weights.astype(BF), value, preferred_element_type=F32)
    return highest, total, summed


def score(queries, keys):
    return lax.dot_general(
        queries, keys, (((1,), (1,)), ((), ())), preferred_element_type=F32
    ) * (1.0 / 16.0)


def split_total(total):
    upper = total.astype(BF).astype(F32)
    return upper, total - upper


def lane_stats(highest, total, first):
    upper, lower = split_total(total)
    rows = highest.shape[0]
    lane = iota((rows, 128), 1)
    place = jnp.where(lane == first, highest, 0.0)
    place = jnp.where(lane == first + 1, upper, place)
    return jnp.where(lane == first + 2, lower, place)


def piece(ref, kv):
    base = kv * 1024
    return jnp.concatenate([ref[base : base + 512], ref[base + 512 : base + 1024]], axis=1)


def branch_kernel(info, q_ref, sent_ref, out_ref):
    zl = info[1]
    length = info[2]
    loaded = q_ref[...].reshape(8, 4, 32, 128)
    blocks = [loaded[:, z].reshape(256, 128) for z in range(4)]
    keys = [piece(sent_ref.at[s], 0) for s in range(4)]
    values = [piece(sent_ref.at[s], 1) for s in range(4)]
    row16 = iota((256, 128), 0) & 31
    for h in range(2):
        queries = jnp.concatenate([blocks[2 * h], blocks[2 * h + 1]], axis=1)
        scores = []
        for s in range(4):
            place = (s * 4 + zl) * 512 + iota((256, 512), 1)
            scores.append(jnp.where(place < length, score(queries, keys[s]), NEG))
        highest, total, summed = softmax_parts(scores, values)
        first = jnp.where(row16 < 16, 0, 64)
        stats = lane_stats(highest, total, first)
        for xc in range(8):
            low = xc * 32
            packed = (stats[low : low + 16] + stats[low + 16 : low + 32]).astype(BF)
            for half in range(2):
                out_ref[xc * 4 + 2 * h + half, 0:32] = summed[
                    low : low + 32, half * 128 : (half + 1) * 128
                ].astype(BF)
                out_ref[xc * 4 + 2 * h + half, 32:48] = packed


def branch_attend(info, arrived, sent):
    full = lambda shape: pl.BlockSpec(shape, lambda i, info: (0,) * len(shape))
    return pl.pallas_call(
        branch_kernel,
        out_shape=jax.ShapeDtypeStruct((32, 48, 128), BF),
        grid_spec=pltpu.PrefetchScalarGridSpec(
            num_scalar_prefetch=1,
            grid=(1,),
            in_specs=[full((32, 32, 128)), full((4, 2080, 128))],
            out_specs=full((32, 48, 128)),
        ),
        compiler_params=params(),
        name="branch_attend",
    )(info, arrived, sent)


def merge_kernel(in_ref, out_ref):
    loaded = in_ref[...].astype(F32).reshape(8, 4, 48, 128)
    data = [loaded[:, z, 0:32] for z in range(4)]
    stats = [loaded[:, z, 32:48] for z in range(4)]

    def column(stat, j):
        return jnp.concatenate([stat[:, :, j : j + 1], stat[:, :, 64 + j : 65 + j]], axis=1)

    peaks = [column(stat, 0) for stat in stats]
    highest = jnp.maximum(jnp.maximum(peaks[0], peaks[1]), jnp.maximum(peaks[2], peaks[3]))
    total = 0.0
    summed = 0.0
    for z in range(4):
        factor = jnp.exp(peaks[z] - highest)
        total = total + factor * (column(stats[z], 1) + column(stats[z], 2))
        summed = summed + factor * data[z]
    highest = highest.reshape(8, 4, 8, 1)
    total = total.reshape(8, 4, 8, 1)
    summed = summed.reshape(8, 4, 8, 128)
    first = (iota((64, 128), 0) >> 4) * 32
    for z in range(4):
        out_ref[z, 0:64] = summed[:, z].reshape(64, 128).astype(BF)
        placed = lane_stats(highest[:, z].reshape(64, 1), total[:, z].reshape(64, 1), first)
        out_ref[z, 64:80] = (
            placed[0:16] + placed[16:32] + placed[32:48] + placed[48:64]
        ).astype(BF)


def merge_node(partials):
    return pl.pallas_call(
        merge_kernel,
        out_shape=jax.ShapeDtypeStruct((4, 80, 128), BF),
        in_specs=[whole((32, 48, 128))],
        out_specs=whole((4, 80, 128)),
        compiler_params=params(),
        name="merge_node",
    )(partials)


def local_kernel(
    info, leaf_ref, lengths_ref, kown, vown, p1, p2, p3, own, root_ref, l0, l1, l2, l3,
    out0, out1, out2, out3, gathered, suffix, outgoing,
):
    y = info[0]
    zl = info[1]
    for s, ref in enumerate((l0, l1, l2, l3)):
        gathered[(zl - s) & 3] = ref[0:128]
    suffix[0] = own[...]
    for s, ref in enumerate((p1, p2, p3)):
        suffix[s + 1] = ref[2048:2304]
    leaf_row = jnp.broadcast_to(leaf_ref[...].astype(F32), (128, 128))
    leaf_col = leaf_row.T
    key_step = (y - (y >> 1)) & 3
    value_step = (y - 2 - (y >> 1)) & 3
    suffix_k = jnp.concatenate([suffix[key_step, 0:128], suffix[key_step, 128:256]], axis=1)
    suffix_v = jnp.concatenate([suffix[value_step, 0:128], suffix[value_step, 128:256]], axis=1)
    root = root_ref[...].reshape(8, 4, 4, 32, 128)
    root_parts = [root[:, :, j].reshape(1024, 128) for j in range(4)]
    root_k = jnp.concatenate(root_parts[0:2], axis=1)
    root_v = jnp.concatenate(root_parts[2:4], axis=1)
    leaf_keys = [kown[...]] + [piece(ref, 0) for ref in (p1, p2, p3)]
    leaf_values = [vown[...]] + [piece(ref, 1) for ref in (p1, p2, p3)]
    token = iota((128, 128), 0)
    key_token = iota((128, 128), 1)
    suffix_ok = (leaf_row == leaf_col) & (key_token <= token) & ((key_token & 3) == zl)
    key_slot = iota((1, 512), 1)
    first = (iota((128, 128), 0) >> 4) * 16
    for h in range(2):
        queries = jnp.concatenate([gathered[2 * h], gathered[2 * h + 1]], axis=1)
        scores = [score(queries, root_k)]
        for s in range(4):
            source = (y - s) & 3
            place = (source * 4 + zl) * 16 + (key_slot & 15)
            key_leaf = jnp.where(place < lengths_ref[...], key_slot >> 4, -1).astype(F32)
            scores.append(
                jnp.where(leaf_col[:, 0:1] == key_leaf, score(queries, leaf_keys[s]), NEG)
            )
        scores.append(jnp.where(suffix_ok, score(queries, suffix_k), NEG))
        highest, total, summed = softmax_parts(scores, [root_v] + leaf_values + [suffix_v])
        stats = lane_stats(highest, total, first)
        packed = stats[0:16]
        for g in range(1, 8):
            packed = packed + stats[g * 16 : (g + 1) * 16]
        for half in range(2):
            outgoing[2 * h + half, 0:128] = summed[:, half * 128 : (half + 1) * 128].astype(BF)
            outgoing[2 * h + half, 128:144] = packed.astype(BF)
    for s, ref in enumerate((out0, out1, out2, out3)):
        ref[...] = outgoing[(zl + s) & 3]


def local_attend(info, leaf, lengths, cache, pieces, own, root, gathered):
    head = pl.BlockSpec((512, 256), lambda i, info: (0, info[0]))
    head_value = pl.BlockSpec((512, 256), lambda i, info: (0, 4 + info[0]))
    full = lambda shape: pl.BlockSpec(shape, lambda i, info: (0,) * len(shape))
    return pl.pallas_call(
        local_kernel,
        out_shape=tuple(jax.ShapeDtypeStruct((144, 128), BF) for _ in range(4)),
        grid_spec=pltpu.PrefetchScalarGridSpec(
            num_scalar_prefetch=1,
            grid=(1,),
            in_specs=[full((1, 128)), full((1, 512)), head, head_value]
            + [full((2304, 128))] * 3
            + [full((256, 128)), full((8, 512, 128))]
            + [full((256, 128))] * 4,
            out_specs=tuple(full((144, 128)) for _ in range(4)),
            scratch_shapes=[
                pltpu.VMEM((4, 128, 128), BF),
                pltpu.VMEM((4, 256, 128), BF),
                pltpu.VMEM((4, 144, 128), BF),
            ],
        ),
        compiler_params=params(),
        cost_estimate=pl.CostEstimate(
            flops=COST_FLOPS, transcendentals=1_000_000, bytes_accessed=8_000_000
        ),
        name="local_attend",
    )(info, leaf, lengths, cache, cache, *pieces, own, root, *gathered)


def final_kernel(slot_ref, branch_ref, l0, l1, l2, l3, out_ref):
    pick = jnp.where(iota((256, 128), 0) == slot_ref[...], 1.0, 0.0).astype(BF)

    def to_tokens(values):
        return lax.dot_general(
            pick, values, (((0,), (0,)), ((), ())), preferred_element_type=F32
        )

    branch = branch_ref[...]
    branch_sum = to_tokens(branch[:, 0:64].reshape(256, 128))
    lane16 = iota((16, 128), 1) >> 5
    spread = []
    for z in range(4):
        stat = branch[z, 64:80].astype(F32)
        for g in range(4):
            spread.append(jnp.where(lane16 == g, stat, 0.0))
    branch_stat = to_tokens(jnp.concatenate(spread, axis=0).astype(BF))
    lane = iota((128, 128), 1)

    def lane_pick(values, hit):
        return jnp.sum(jnp.where(hit, values, 0.0), axis=1, keepdims=True)

    column = lane & 31
    peaks = [lane_pick(branch_stat, column == 0)]
    totals = [lane_pick(branch_stat, (column == 1) | (column == 2))]
    sums = [branch_sum]
    first = (iota((128, 128), 0) >> 4) * 16
    for ref in (l0, l1, l2, l3):
        sums.append(ref[0:128].astype(F32))
        stat = ref[128:144].astype(F32)
        stat = jnp.concatenate([stat] * 8, axis=0)
        peaks.append(lane_pick(stat, lane == first))
        totals.append(lane_pick(stat, (lane == first + 1) | (lane == first + 2)))
    highest = peaks[0]
    for peak in peaks[1:]:
        highest = jnp.maximum(highest, peak)
    total = 0.0
    summed = 0.0
    for peak, part, value in zip(peaks, totals, sums):
        factor = jnp.exp(peak - highest)
        total = total + factor * part
        summed = summed + factor * value
    out_ref[...] = (summed / total).astype(BF)


def finish(slot, branch, parts):
    return pl.pallas_call(
        final_kernel,
        out_shape=jax.ShapeDtypeStruct((128, 128), BF),
        in_specs=[whole((1, 128)), whole((4, 80, 128))] + [whole((144, 128))] * 4,
        out_specs=whole((128, 128)),
        compiler_params=params(),
        name="finish",
    )(slot, branch, *parts)


def shift(values, axis, step):
    return lax.ppermute(values, axis, [(i, (i + step) % 4) for i in range(4)])


def exchange(values, axis):
    return lax.all_to_all(values, axis, split_axis=0, concat_axis=0, tiled=True)


def on_device(
    queries, suffix_cache, suffix_leaf, leaf_parent, root_cache,
    branch_cache, branch_length, leaf_cache, leaf_length,
):
    y = lax.axis_index("y")
    zl = lax.axis_index("zl")
    info = jnp.stack([y, zl, branch_length[0]]).astype(jnp.int32)
    branch_rows = branch_cache.reshape(512, 2048)
    leaf_rows = leaf_cache.reshape(512, 2048)

    tie = lax.optimization_barrier
    routed, slot, sent = first_stage(
        leaf_parent, suffix_leaf, queries, root_cache, branch_rows
    )
    sent = exchange(sent, "y")
    mine = jnp.concatenate([queries, suffix_cache], axis=0)
    gathered = [mine] + [shift(mine, "zl", s + 1) for s in range(3)]
    packed = pack_leaf(info, leaf_rows, gathered)
    own = packed[3]
    onward = jnp.concatenate(
        [routed, jnp.broadcast_to(sent[:, 2048:2080].reshape(1, 128, 128), (4, 128, 128))], axis=1
    )
    onward, packed = tie((onward, packed))
    arrived = exchange(onward, "zh")
    leaf_in = [shift(packed[s], "y", s + 1) for s in range(3)]

    onward = arrived[:, 0:64].reshape(4, 8, 8, 128).transpose(1, 0, 2, 3).reshape(8, 1, 32, 128)
    onward = jnp.broadcast_to(onward, (8, 4, 32, 128)).reshape(32, 32, 128)
    node_queries = exchange(onward, XCZ)

    root = arrived[:, 64:192].reshape(4, 4, 4, 8, 128).transpose(1, 2, 0, 3, 4)
    root_all = lax.all_gather(root.reshape(512, 128), XC, axis=0, tiled=False)

    partials = branch_attend(info, node_queries, sent)
    returned = exchange(partials, XCZ)
    merged = merge_node(returned)
    lengths = jnp.repeat(leaf_length, 16).reshape(1, 512)
    local = local_attend(
        info, suffix_leaf, lengths, leaf_rows, leaf_in, own, root_all, gathered
    )
    merged, local = tie((merged, local))
    back = exchange(merged, "zh")
    parts = [local[0]] + [shift(local[s + 1], "zl", s + 1) for s in range(3)]
    return finish(slot, back, parts)


def solution(mesh):
    fine = Mesh(mesh.devices.reshape(4, 4, 2, 4, 4), ("zh", "x", "core", "y", "zl"))
    in_specs = (
        P(ROW, COL),
        P(ROW, COL),
        P(ROW, None),
        P(ROW, None),
        P(ROW + COL, None),
        P(ROW, COL, None),
        P(ROW),
        P(ROW, COL, None),
        P(ROW),
    )
    return jax.shard_map(
        on_device, mesh=fine, in_specs=in_specs, out_specs=P(ROW, COL), check_vma=False
    )
```

```python
import jax
import jax.numpy as jnp
from jax import lax
from jax.experimental import pallas as pl
from jax.experimental.pallas import tpu as pltpu
from jax.sharding import Mesh, PartitionSpec as P

ROW = ("zh", "x", "core")
COL = ("y", "zl")
XC = ("x", "core")
XCZ = ("x", "core", "zl")
BF = jnp.bfloat16
F32 = jnp.float32
NEG = -1e30
FLOOR = -1e29
COST_FLOPS = 15_000_000_000
LOCAL_FLOPS = 30_000_000_000
LENGTH_FLOPS = 6_000_000_000
VMEM_LIMIT = 50 * 1024 * 1024


def iota(shape, dim):
    return lax.broadcasted_iota(jnp.int32, shape, dim)


def whole(shape):
    return pl.BlockSpec(shape, lambda: (0,) * len(shape))


SMEM = pl.BlockSpec(memory_space=pltpu.SMEM)
HBM = pl.BlockSpec(memory_space=pltpu.HBM)


def in_hbm(value):
    return pltpu.with_memory_space_constraint(value, pltpu.HBM)


def params():
    return pltpu.CompilerParams(vmem_limit_bytes=VMEM_LIMIT)


def first_kernel(
    parent, leaf_hbm, q_hbm, root_hbm, suffix_hbm, out_ref, slot_ref, split_ref,
    leaf_ref, q_ref, root_ref, suffix_ref, sems,
):
    copies = [
        pltpu.make_async_copy(source, target, sems.at[i])
        for i, (source, target) in enumerate(
            ((root_hbm, root_ref), (leaf_hbm, leaf_ref), (q_hbm, q_ref), (suffix_hbm, suffix_ref))
        )
    ]
    for copy in copies:
        copy.start()
    for copy in copies:
        copy.wait()
    root = root_ref[...].astype(F32)
    for target in range(4):
        lanes = [kv * 1024 + target * 256 + half * 128 for kv in range(2) for half in range(2)]
        split_ref[target, 32:160] = suffix_ref[...]
        split_ref[target, 0:32] = jnp.concatenate([root[:, l : l + 128] for l in lanes], axis=0).astype(BF)
    leaf = leaf_ref[...]
    across = jnp.broadcast_to(leaf.astype(F32), (128, 128))
    down = across.T
    before = iota((128, 128), 0) < iota((128, 128), 1)
    rank = jnp.sum(jnp.where((across == down) & before, 1.0, 0.0), axis=0, keepdims=True)
    node = jnp.zeros((1, 128), jnp.int32)
    for leaf_id in range(32):
        node = jnp.where(leaf == leaf_id, parent[0, leaf_id], node)
    slot = node * 8 + rank.astype(jnp.int32)
    slot_ref[...] = slot
    pick = jnp.where(iota((256, 128), 0) == slot, 1.0, 0.0).astype(BF)
    routed = jnp.dot(pick, q_ref[...], preferred_element_type=F32).astype(BF)
    out_ref[...] = routed.reshape(4, 64, 128)


def first_stage(parent, leaf, queries, root, suffix):
    return pl.pallas_call(
        first_kernel,
        out_shape=(
            jax.ShapeDtypeStruct((4, 64, 128), BF),
            jax.ShapeDtypeStruct((1, 128), jnp.int32),
            jax.ShapeDtypeStruct((4, 160, 128), BF),
        ),
        in_specs=[SMEM, HBM, HBM, HBM, HBM],
        out_specs=(whole((4, 64, 128)), whole((1, 128)), whole((4, 160, 128))),
        scratch_shapes=[
            pltpu.VMEM((1, 128), jnp.int32),
            pltpu.VMEM((128, 128), BF),
            pltpu.VMEM((8, 2048), BF),
            pltpu.VMEM((128, 128), BF),
            pltpu.SemaphoreType.DMA((4,)),
        ],
        compiler_params=params(),
        name="first_stage",
    )(parent, in_hbm(leaf), in_hbm(queries), in_hbm(root), in_hbm(suffix))


def pack_kernel(info, branch, leaf, sent1, sent2, sent3, branch_buf, leaf_buf, loads, stores):
    pairs = ((branch, branch_buf), (leaf, leaf_buf))
    fetches = [
        pltpu.make_async_copy(cache, buf, loads.at[i]) for i, (cache, buf) in enumerate(pairs)
    ]
    for fetch in fetches:
        fetch.start()
    moves = []
    for i, (_, buf) in enumerate(pairs):
        fetches[i].wait()
        for s, sent in enumerate((sent1, sent2, sent3)):
            target = (info[0] + (s + 1)) & 3
            for part in range(4):
                start = (part // 2) * 1024 + (part % 2) * 128
                lane = pl.multiple_of(target * 256 + start, 128)
                moves.append(
                    pltpu.make_async_copy(
                        buf.at[:, pl.ds(lane, 128)],
                        sent.at[pl.ds(i * 2048 + part * 512, 512), :],
                        stores.at[i, s, part],
                    )
                )
                moves[-1].start()
    for move in moves:
        move.wait()


def pack_caches(info, branch, leaf):
    return pl.pallas_call(
        pack_kernel,
        out_shape=tuple(jax.ShapeDtypeStruct((4096, 128), BF) for _ in range(3)),
        in_specs=[SMEM, HBM, HBM],
        out_specs=(HBM, HBM, HBM),
        scratch_shapes=[
            pltpu.VMEM((512, 2048), BF),
            pltpu.VMEM((512, 2048), BF),
            pltpu.SemaphoreType.DMA((2,)),
            pltpu.SemaphoreType.DMA((2, 3, 4)),
        ],
        compiler_params=params(),
        name="pack_caches",
    )(info, in_hbm(branch), in_hbm(leaf))


def lengths_kernel(lengths, out):
    leaf = iota((1, 512), 1) >> 4
    row = jnp.zeros((1, 512), jnp.int32)
    for i in range(32):
        row = jnp.where(leaf == i, lengths[i], row)
    out[...] = row


def key_lengths(lengths):
    return pl.pallas_call(
        lengths_kernel,
        out_shape=jax.ShapeDtypeStruct((1, 512), jnp.int32),
        in_specs=[SMEM],
        out_specs=whole((1, 512)),
        compiler_params=params(),
        cost_estimate=pl.CostEstimate(
            flops=LENGTH_FLOPS, transcendentals=1_000_000, bytes_accessed=8_000_000
        ),
        name="key_lengths",
    )(lengths)


def arrive_kernel(info, p1, p2, p3, out):
    for i in range(3):
        out[i] = info[i]


def arrive(info, pieces):
    return pl.pallas_call(
        arrive_kernel,
        out_shape=jax.ShapeDtypeStruct((3,), jnp.int32),
        in_specs=[SMEM, HBM, HBM, HBM],
        out_specs=SMEM,
        compiler_params=params(),
        cost_estimate=pl.CostEstimate(
            flops=COST_FLOPS, transcendentals=1_000_000, bytes_accessed=8_000_000
        ),
        name="arrive",
    )(info, *pieces)


def softmax_parts(scores, values):
    highest = scores[0].max(axis=1, keepdims=True)
    for part in scores[1:]:
        highest = jnp.maximum(highest, part.max(axis=1, keepdims=True))
    highest = jnp.maximum(highest, FLOOR).astype(BF).astype(F32)
    total = 0.0
    summed = 0.0
    for part, value in zip(scores, values):
        weights = jnp.exp(part - highest)
        total = total + jnp.sum(weights, axis=1, keepdims=True)
        summed = summed + jnp.dot(weights.astype(BF), value, preferred_element_type=F32)
    return highest, total, summed


def score(queries, keys):
    return lax.dot_general(
        queries, keys, (((1,), (1,)), ((), ())), preferred_element_type=F32
    ) * (1.0 / 16.0)


def split_total(total):
    upper = total.astype(BF).astype(F32)
    return upper, total - upper


def lane_stats(highest, total, first):
    upper, lower = split_total(total)
    rows = highest.shape[0]
    lane = iota((rows, 128), 1)
    place = jnp.where(lane == first, highest, 0.0)
    place = jnp.where(lane == first + 1, upper, place)
    return jnp.where(lane == first + 2, lower, place)


def piece(ref, kv):
    base = kv * 1024
    return jnp.concatenate([ref[base : base + 512], ref[base + 512 : base + 1024]], axis=1)


def branch_kernel(info, q_ref, kown, vown, p1, p2, p3, out_ref):
    y = info[0]
    zl = info[1]
    length = info[2]
    loaded = q_ref[...].reshape(8, 4, 32, 128)
    blocks = [loaded[:, z].reshape(256, 128) for z in range(4)]
    keys = [kown[...]] + [piece(ref, 0) for ref in (p1, p2, p3)]
    values = [vown[...]] + [piece(ref, 1) for ref in (p1, p2, p3)]
    row16 = iota((256, 128), 0) & 31
    for h in range(2):
        queries = jnp.concatenate([blocks[2 * h], blocks[2 * h + 1]], axis=1)
        scores = []
        for s in range(4):
            place = (((y - s) & 3) * 4 + zl) * 512 + iota((256, 512), 1)
            scores.append(jnp.where(place < length, score(queries, keys[s]), NEG))
        highest, total, summed = softmax_parts(scores, values)
        first = jnp.where(row16 < 16, 0, 64)
        stats = lane_stats(highest, total, first)
        for xc in range(8):
            low = xc * 32
            packed = (stats[low : low + 16] + stats[low + 16 : low + 32]).astype(BF)
            for half in range(2):
                out_ref[xc * 4 + 2 * h + half, 0:32] = summed[
                    low : low + 32, half * 128 : (half + 1) * 128
                ].astype(BF)
                out_ref[xc * 4 + 2 * h + half, 32:48] = packed


def branch_attend(info, arrived, cache, pieces):
    head = pl.BlockSpec((512, 256), lambda i, info: (0, info[0]))
    head_value = pl.BlockSpec((512, 256), lambda i, info: (0, 4 + info[0]))
    full = lambda shape: pl.BlockSpec(shape, lambda i, info: (0,) * len(shape))
    return pl.pallas_call(
        branch_kernel,
        out_shape=jax.ShapeDtypeStruct((32, 48, 128), BF),
        grid_spec=pltpu.PrefetchScalarGridSpec(
            num_scalar_prefetch=1,
            grid=(1,),
            in_specs=[full((32, 32, 128)), head, head_value] + [pl.BlockSpec((2048, 128), lambda i, info: (0, 0))] * 3,
            out_specs=full((32, 48, 128)),
        ),
        compiler_params=params(),
        name="branch_attend",
    )(info, arrived, cache, cache, *pieces)


def merge_kernel(in_ref, out_ref):
    loaded = in_ref[...].astype(F32).reshape(8, 4, 48, 128)
    data = [loaded[:, z, 0:32] for z in range(4)]
    stats = [loaded[:, z, 32:48] for z in range(4)]

    def column(stat, j):
        return jnp.concatenate([stat[:, :, j : j + 1], stat[:, :, 64 + j : 65 + j]], axis=1)

    peaks = [column(stat, 0) for stat in stats]
    highest = jnp.maximum(jnp.maximum(peaks[0], peaks[1]), jnp.maximum(peaks[2], peaks[3]))
    total = 0.0
    summed = 0.0
    for z in range(4):
        factor = jnp.exp(peaks[z] - highest)
        total = total + factor * (column(stats[z], 1) + column(stats[z], 2))
        summed = summed + factor * data[z]
    highest = highest.reshape(8, 4, 8, 1)
    total = total.reshape(8, 4, 8, 1)
    summed = summed.reshape(8, 4, 8, 128)
    first = (iota((64, 128), 0) >> 4) * 32
    for z in range(4):
        out_ref[z, 0:64] = summed[:, z].reshape(64, 128).astype(BF)
        placed = lane_stats(highest[:, z].reshape(64, 1), total[:, z].reshape(64, 1), first)
        out_ref[z, 64:80] = (
            placed[0:16] + placed[16:32] + placed[32:48] + placed[48:64]
        ).astype(BF)


def merge_node(partials):
    return pl.pallas_call(
        merge_kernel,
        out_shape=jax.ShapeDtypeStruct((4, 80, 128), BF),
        in_specs=[whole((32, 48, 128))],
        out_specs=whole((4, 80, 128)),
        compiler_params=params(),
        name="merge_node",
    )(partials)


def local_kernel(
    info, leaf_ref, lengths_ref, kown, vown, p1, p2, p3, root_ref, l0, l1, l2, l3,
    out0, out1, out2, out3, gathered, outgoing,
):
    y = info[0]
    zl = info[1]
    for s, ref in enumerate((l0, l1, l2, l3)):
        gathered[(zl - s) & 3] = ref[...]
    leaf_row = jnp.broadcast_to(leaf_ref[...].astype(F32), (128, 128))
    leaf_col = leaf_row.T
    first_half = (y & 1) * 2
    suffix_k = jnp.concatenate(
        [gathered[first_half, 128:256], gathered[first_half + 1, 128:256]], axis=1
    )
    suffix_v = jnp.concatenate(
        [gathered[first_half, 256:384], gathered[first_half + 1, 256:384]], axis=1
    )
    root = root_ref[...].reshape(8, 4, 4, 32, 128)
    root_parts = [root[:, :, j].reshape(1024, 128) for j in range(4)]
    root_k = jnp.concatenate(root_parts[0:2], axis=1)
    root_v = jnp.concatenate(root_parts[2:4], axis=1)
    leaf_keys = [kown[...]] + [piece(ref, 0) for ref in (p1, p2, p3)]
    leaf_values = [vown[...]] + [piece(ref, 1) for ref in (p1, p2, p3)]
    token = iota((128, 128), 0)
    key_token = iota((128, 128), 1)
    suffix_ok = (leaf_row == leaf_col) & (key_token <= token) & ((key_token & 3) == zl)
    key_slot = iota((1, 512), 1)
    first = (iota((128, 128), 0) >> 4) * 16
    for h in range(2):
        queries = jnp.concatenate([gathered[2 * h, 0:128], gathered[2 * h + 1, 0:128]], axis=1)
        scores = [score(queries, root_k)]
        for s in range(4):
            source = (y - s) & 3
            place = (source * 4 + zl) * 16 + (key_slot & 15)
            key_leaf = jnp.where(place < lengths_ref[...], key_slot >> 4, -1).astype(F32)
            scores.append(
                jnp.where(leaf_col[:, 0:1] == key_leaf, score(queries, leaf_keys[s]), NEG)
            )
        scores.append(jnp.where(suffix_ok, score(queries, suffix_k), NEG))
        highest, total, summed = softmax_parts(scores, [root_v] + leaf_values + [suffix_v])
        stats = lane_stats(highest, total, first)
        packed = stats[0:16]
        for g in range(1, 8):
            packed = packed + stats[g * 16 : (g + 1) * 16]
        for half in range(2):
            outgoing[2 * h + half, 0:128] = summed[:, half * 128 : (half + 1) * 128].astype(BF)
            outgoing[2 * h + half, 128:144] = packed.astype(BF)
    for s, ref in enumerate((out0, out1, out2, out3)):
        ref[...] = outgoing[(zl + s) & 3]


def local_attend(info, leaf, lengths, cache, pieces, root, gathered):
    head = pl.BlockSpec((512, 256), lambda i, info: (0, info[0]))
    head_value = pl.BlockSpec((512, 256), lambda i, info: (0, 4 + info[0]))
    full = lambda shape: pl.BlockSpec(shape, lambda i, info: (0,) * len(shape))
    return pl.pallas_call(
        local_kernel,
        out_shape=tuple(jax.ShapeDtypeStruct((144, 128), BF) for _ in range(4)),
        grid_spec=pltpu.PrefetchScalarGridSpec(
            num_scalar_prefetch=1,
            grid=(1,),
            in_specs=[full((1, 128)), full((1, 512)), head, head_value]
            + [pl.BlockSpec((2048, 128), lambda i, info: (1, 0))] * 3
            + [full((8, 512, 128))]
            + [full((384, 128))] * 4,
            out_specs=tuple(full((144, 128)) for _ in range(4)),
            scratch_shapes=[pltpu.VMEM((4, 384, 128), BF), pltpu.VMEM((4, 144, 128), BF)],
        ),
        compiler_params=params(),
        cost_estimate=pl.CostEstimate(
            flops=LOCAL_FLOPS, transcendentals=1_000_000, bytes_accessed=8_000_000
        ),
        name="local_attend",
    )(info, leaf, lengths, cache, cache, *pieces, in_hbm(root), *gathered)


def final_kernel(slot_ref, branch_ref, l0, l1, l2, l3, out_ref):
    pick = jnp.where(iota((256, 128), 0) == slot_ref[...], 1.0, 0.0).astype(BF)

    def to_tokens(values):
        return lax.dot_general(
            pick, values, (((0,), (0,)), ((), ())), preferred_element_type=F32
        )

    branch = branch_ref[...]
    branch_sum = to_tokens(branch[:, 0:64].reshape(256, 128))
    lane16 = iota((16, 128), 1) >> 5
    spread = []
    for z in range(4):
        stat = branch[z, 64:80].astype(F32)
        for g in range(4):
            spread.append(jnp.where(lane16 == g, stat, 0.0))
    branch_stat = to_tokens(jnp.concatenate(spread, axis=0).astype(BF))
    lane = iota((128, 128), 1)

    def lane_pick(values, hit):
        return jnp.sum(jnp.where(hit, values, 0.0), axis=1, keepdims=True)

    column = lane & 31
    peaks = [lane_pick(branch_stat, column == 0)]
    totals = [lane_pick(branch_stat, (column == 1) | (column == 2))]
    sums = [branch_sum]
    first = (iota((128, 128), 0) >> 4) * 16
    for ref in (l0, l1, l2, l3):
        sums.append(ref[0:128].astype(F32))
        stat = ref[128:144].astype(F32)
        stat = jnp.concatenate([stat] * 8, axis=0)
        peaks.append(lane_pick(stat, lane == first))
        totals.append(lane_pick(stat, (lane == first + 1) | (lane == first + 2)))
    highest = peaks[0]
    for peak in peaks[1:]:
        highest = jnp.maximum(highest, peak)
    total = 0.0
    summed = 0.0
    for peak, part, value in zip(peaks, totals, sums):
        factor = jnp.exp(peak - highest)
        total = total + factor * part
        summed = summed + factor * value
    out_ref[...] = (summed / total).astype(BF)


def finish(slot, branch, parts):
    return pl.pallas_call(
        final_kernel,
        out_shape=jax.ShapeDtypeStruct((128, 128), BF),
        in_specs=[whole((1, 128)), whole((4, 80, 128))] + [whole((144, 128))] * 4,
        out_specs=whole((128, 128)),
        compiler_params=params(),
        name="finish",
    )(slot, branch, *parts)


def shift(values, axis, step):
    return lax.ppermute(values, axis, [(i, (i + step) % 4) for i in range(4)])


def exchange(values, axis):
    return lax.all_to_all(values, axis, split_axis=0, concat_axis=0, tiled=True)


def on_device(
    queries, suffix_cache, suffix_leaf, leaf_parent, root_cache,
    branch_cache, branch_length, leaf_cache, leaf_length,
):
    y = lax.axis_index("y")
    zl = lax.axis_index("zl")
    info = jnp.stack([y, zl, branch_length[0]]).astype(jnp.int32)
    branch_rows = branch_cache.reshape(512, 2048)
    leaf_rows = leaf_cache.reshape(512, 2048)

    tie = lax.optimization_barrier
    routed, slot, split = first_stage(
        leaf_parent, suffix_leaf, queries, root_cache, suffix_cache
    )
    own = exchange(split, "y")
    sent = pack_caches(info, branch_rows, leaf_rows)
    pieces = [shift(sent[s], "y", s + 1) for s in range(3)]
    onward = jnp.concatenate(
        [routed, jnp.broadcast_to(own[:, 0:32].reshape(1, 128, 128), (4, 128, 128))], axis=1
    )
    arrived = exchange(onward, "zh")
    def chosen(source):
        return lax.dynamic_index_in_dim(own, source, 0, keepdims=False)[32:160]

    mine = jnp.concatenate([queries, chosen(y >> 1), chosen(2 + (y >> 1))], axis=0)
    gathered = [mine] + [shift(mine, "zl", s + 1) for s in range(3)]
    arrived, lengths, gathered[1], gathered[2] = tie((arrived, key_lengths(leaf_length), gathered[1], gathered[2]))

    onward = arrived[:, 0:64].reshape(4, 8, 8, 128).transpose(1, 0, 2, 3).reshape(8, 1, 32, 128)
    onward = jnp.broadcast_to(onward, (8, 4, 32, 128)).reshape(32, 32, 128)
    root = arrived[:, 64:192].reshape(4, 4, 4, 8, 128).transpose(1, 2, 0, 3, 4)
    onward, root = tie((onward, root.reshape(512, 128)))
    root_all = lax.all_gather(root, XC, axis=0, tiled=False)
    node_queries = exchange(onward, XCZ)

    partials = branch_attend(arrive(info, pieces), node_queries, branch_rows, pieces)
    returned = exchange(partials, XCZ)
    merged = merge_node(returned)
    local = local_attend(info, suffix_leaf, lengths, leaf_rows, pieces, root_all, gathered)
    merged, own_part = tie((merged, local[0]))
    back = exchange(merged, "zh")
    parts = [own_part] + [shift(local[s + 1], "zl", s + 1) for s in range(3)]
    return finish(slot, back, parts)


def solution(mesh):
    fine = Mesh(mesh.devices.reshape(4, 4, 2, 4, 4), ("zh", "x", "core", "y", "zl"))
    in_specs = (
        P(ROW, COL),
        P(ROW, COL),
        P(ROW, None),
        P(ROW, None),
        P(ROW + COL, None),
        P(ROW, COL, None),
        P(ROW),
        P(ROW, COL, None),
        P(ROW),
    )
    return jax.shard_map(
        on_device, mesh=fine, in_specs=in_specs, out_specs=P(ROW, COL), check_vma=False
    )
```

```python
import jax
import jax.numpy as jnp
from jax import lax
from jax.experimental import pallas as pl
from jax.experimental.pallas import tpu as pltpu
from jax.sharding import Mesh, PartitionSpec as P

ROW = ("zh", "x", "core")
COL = ("y", "zl")
XC = ("x", "core")
XCZ = ("x", "core", "zl")
BF = jnp.bfloat16
F32 = jnp.float32
NEG = -1e30
FLOOR = -1e29
COST_FLOPS = 15_000_000_000
LOCAL_FLOPS = 30_000_000_000
LENGTH_FLOPS = 6_000_000_000
VMEM_LIMIT = 32 * 1024 * 1024


def iota(shape, dim):
    return lax.broadcasted_iota(jnp.int32, shape, dim)


def whole(shape):
    return pl.BlockSpec(shape, lambda: (0,) * len(shape))


SMEM = pl.BlockSpec(memory_space=pltpu.SMEM)
HBM = pl.BlockSpec(memory_space=pltpu.HBM)


def in_hbm(value):
    return pltpu.with_memory_space_constraint(value, pltpu.HBM)


def params():
    return pltpu.CompilerParams(vmem_limit_bytes=VMEM_LIMIT)


def first_kernel(
    parent, leaf_hbm, q_hbm, root_hbm, suffix_hbm, out_ref, slot_ref, split_ref,
    leaf_ref, q_ref, root_ref, suffix_ref, sems,
):
    copies = [
        pltpu.make_async_copy(source, target, sems.at[i])
        for i, (source, target) in enumerate(
            ((root_hbm, root_ref), (leaf_hbm, leaf_ref), (q_hbm, q_ref), (suffix_hbm, suffix_ref))
        )
    ]
    for copy in copies:
        copy.start()
    for copy in copies:
        copy.wait()
    root = root_ref[...].astype(F32)
    for target in range(4):
        lanes = [kv * 1024 + target * 256 + half * 128 for kv in range(2) for half in range(2)]
        split_ref[target, 32:160] = suffix_ref[...]
        split_ref[target, 0:32] = jnp.concatenate([root[:, l : l + 128] for l in lanes], axis=0).astype(BF)
    leaf = leaf_ref[...]
    across = jnp.broadcast_to(leaf.astype(F32), (128, 128))
    down = across.T
    before = iota((128, 128), 0) < iota((128, 128), 1)
    rank = jnp.sum(jnp.where((across == down) & before, 1.0, 0.0), axis=0, keepdims=True)
    node = jnp.zeros((1, 128), jnp.int32)
    for leaf_id in range(32):
        node = jnp.where(leaf == leaf_id, parent[0, leaf_id], node)
    slot = node * 8 + rank.astype(jnp.int32)
    slot_ref[...] = slot
    pick = jnp.where(iota((256, 128), 0) == slot, 1.0, 0.0).astype(BF)
    routed = jnp.dot(pick, q_ref[...], preferred_element_type=F32).astype(BF)
    out_ref[...] = routed.reshape(4, 64, 128)


def first_stage(parent, leaf, queries, root, suffix):
    return pl.pallas_call(
        first_kernel,
        out_shape=(
            jax.ShapeDtypeStruct((4, 64, 128), BF),
            jax.ShapeDtypeStruct((1, 128), jnp.int32),
            jax.ShapeDtypeStruct((4, 160, 128), BF),
        ),
        in_specs=[SMEM, HBM, HBM, HBM, HBM],
        out_specs=(whole((4, 64, 128)), whole((1, 128)), whole((4, 160, 128))),
        scratch_shapes=[
            pltpu.VMEM((1, 128), jnp.int32),
            pltpu.VMEM((128, 128), BF),
            pltpu.VMEM((8, 2048), BF),
            pltpu.VMEM((128, 128), BF),
            pltpu.SemaphoreType.DMA((4,)),
        ],
        compiler_params=params(),
        name="first_stage",
    )(parent, in_hbm(leaf), in_hbm(queries), in_hbm(root), in_hbm(suffix))


def pack_kernel(info, branch, leaf, sent1, sent2, sent3, branch_buf, leaf_buf, loads, stores):
    pairs = ((branch, branch_buf), (leaf, leaf_buf))
    fetches = [
        pltpu.make_async_copy(cache, buf, loads.at[i]) for i, (cache, buf) in enumerate(pairs)
    ]
    for fetch in fetches:
        fetch.start()
    moves = []
    for i, (_, buf) in enumerate(pairs):
        fetches[i].wait()
        for s, sent in enumerate((sent1, sent2, sent3)):
            target = (info[0] + (s + 1)) & 3
            for part in range(4):
                start = (part // 2) * 1024 + (part % 2) * 128
                lane = pl.multiple_of(target * 256 + start, 128)
                moves.append(
                    pltpu.make_async_copy(
                        buf.at[:, pl.ds(lane, 128)],
                        sent.at[pl.ds(i * 2048 + part * 512, 512), :],
                        stores.at[i, s, part],
                    )
                )
                moves[-1].start()
    for move in moves:
        move.wait()


def pack_caches(info, branch, leaf):
    return pl.pallas_call(
        pack_kernel,
        out_shape=tuple(jax.ShapeDtypeStruct((4096, 128), BF) for _ in range(3)),
        in_specs=[SMEM, HBM, HBM],
        out_specs=(HBM, HBM, HBM),
        scratch_shapes=[
            pltpu.VMEM((512, 2048), BF),
            pltpu.VMEM((512, 2048), BF),
            pltpu.SemaphoreType.DMA((2,)),
            pltpu.SemaphoreType.DMA((2, 3, 4)),
        ],
        compiler_params=params(),
        name="pack_caches",
    )(info, in_hbm(branch), in_hbm(leaf))


def lengths_kernel(lengths, out):
    leaf = iota((1, 512), 1) >> 4
    row = jnp.zeros((1, 512), jnp.int32)
    for i in range(32):
        row = jnp.where(leaf == i, lengths[i], row)
    out[...] = row


def key_lengths(lengths):
    return pl.pallas_call(
        lengths_kernel,
        out_shape=jax.ShapeDtypeStruct((1, 512), jnp.int32),
        in_specs=[SMEM],
        out_specs=whole((1, 512)),
        compiler_params=params(),
        cost_estimate=pl.CostEstimate(
            flops=LENGTH_FLOPS, transcendentals=1_000_000, bytes_accessed=8_000_000
        ),
        name="key_lengths",
    )(lengths)


def arrive_kernel(info, p1, p2, p3, out):
    for i in range(3):
        out[i] = info[i]


def arrive(info, pieces):
    return pl.pallas_call(
        arrive_kernel,
        out_shape=jax.ShapeDtypeStruct((3,), jnp.int32),
        in_specs=[SMEM, HBM, HBM, HBM],
        out_specs=SMEM,
        compiler_params=params(),
        cost_estimate=pl.CostEstimate(
            flops=COST_FLOPS, transcendentals=1_000_000, bytes_accessed=8_000_000
        ),
        name="arrive",
    )(info, *pieces)


def softmax_parts(scores, values):
    highest = scores[0].max(axis=1, keepdims=True)
    for part in scores[1:]:
        highest = jnp.maximum(highest, part.max(axis=1, keepdims=True))
    highest = jnp.maximum(highest, FLOOR).astype(BF).astype(F32)
    total = 0.0
    summed = 0.0
    for part, value in zip(scores, values):
        weights = jnp.exp(part - highest)
        total = total + jnp.sum(weights, axis=1, keepdims=True)
        summed = summed + jnp.dot(weights.astype(BF), value, preferred_element_type=F32)
    return highest, total, summed


def score(queries, keys):
    return lax.dot_general(
        queries, keys, (((1,), (1,)), ((), ())), preferred_element_type=F32
    ) * (1.0 / 16.0)


def split_total(total):
    upper = total.astype(BF).astype(F32)
    return upper, total - upper


def lane_stats(highest, total, first):
    upper, lower = split_total(total)
    rows = highest.shape[0]
    lane = iota((rows, 128), 1)
    place = jnp.where(lane == first, highest, 0.0)
    place = jnp.where(lane == first + 1, upper, place)
    return jnp.where(lane == first + 2, lower, place)


def piece(ref, kv):
    base = kv * 1024
    return jnp.concatenate([ref[base : base + 512], ref[base + 512 : base + 1024]], axis=1)


def branch_kernel(info, q_ref, kown, vown, p1, p2, p3, out_ref):
    y = info[0]
    zl = info[1]
    length = info[2]
    loaded = q_ref[...].reshape(8, 4, 32, 128)
    blocks = [loaded[:, z].reshape(256, 128) for z in range(4)]
    keys = [kown[...]] + [piece(ref, 0) for ref in (p1, p2, p3)]
    values = [vown[...]] + [piece(ref, 1) for ref in (p1, p2, p3)]
    row16 = iota((256, 128), 0) & 31
    for h in range(2):
        queries = jnp.concatenate([blocks[2 * h], blocks[2 * h + 1]], axis=1)
        scores = []
        for s in range(4):
            place = (((y - s) & 3) * 4 + zl) * 512 + iota((256, 512), 1)
            scores.append(jnp.where(place < length, score(queries, keys[s]), NEG))
        highest, total, summed = softmax_parts(scores, values)
        first = jnp.where(row16 < 16, 0, 64)
        stats = lane_stats(highest, total, first)
        for xc in range(8):
            low = xc * 32
            packed = (stats[low : low + 16] + stats[low + 16 : low + 32]).astype(BF)
            for half in range(2):
                out_ref[xc * 4 + 2 * h + half, 0:32] = summed[
                    low : low + 32, half * 128 : (half + 1) * 128
                ].astype(BF)
                out_ref[xc * 4 + 2 * h + half, 32:48] = packed


def branch_attend(info, arrived, cache, pieces):
    head = pl.BlockSpec((512, 256), lambda i, info: (0, info[0]))
    head_value = pl.BlockSpec((512, 256), lambda i, info: (0, 4 + info[0]))
    full = lambda shape: pl.BlockSpec(shape, lambda i, info: (0,) * len(shape))
    return pl.pallas_call(
        branch_kernel,
        out_shape=jax.ShapeDtypeStruct((32, 48, 128), BF),
        grid_spec=pltpu.PrefetchScalarGridSpec(
            num_scalar_prefetch=1,
            grid=(1,),
            in_specs=[full((32, 32, 128)), head, head_value] + [pl.BlockSpec((2048, 128), lambda i, info: (0, 0))] * 3,
            out_specs=full((32, 48, 128)),
        ),
        compiler_params=params(),
        name="branch_attend",
    )(info, arrived, cache, cache, *pieces)


def merge_kernel(in_ref, out_ref):
    loaded = in_ref[...].astype(F32).reshape(8, 4, 48, 128)
    data = [loaded[:, z, 0:32] for z in range(4)]
    stats = [loaded[:, z, 32:48] for z in range(4)]

    def column(stat, j):
        return jnp.concatenate([stat[:, :, j : j + 1], stat[:, :, 64 + j : 65 + j]], axis=1)

    peaks = [column(stat, 0) for stat in stats]
    highest = jnp.maximum(jnp.maximum(peaks[0], peaks[1]), jnp.maximum(peaks[2], peaks[3]))
    total = 0.0
    summed = 0.0
    for z in range(4):
        factor = jnp.exp(peaks[z] - highest)
        total = total + factor * (column(stats[z], 1) + column(stats[z], 2))
        summed = summed + factor * data[z]
    highest = highest.reshape(8, 4, 8, 1)
    total = total.reshape(8, 4, 8, 1)
    summed = summed.reshape(8, 4, 8, 128)
    first = (iota((64, 128), 0) >> 4) * 32
    for z in range(4):
        out_ref[z, 0:64] = summed[:, z].reshape(64, 128).astype(BF)
        placed = lane_stats(highest[:, z].reshape(64, 1), total[:, z].reshape(64, 1), first)
        out_ref[z, 64:80] = (
            placed[0:16] + placed[16:32] + placed[32:48] + placed[48:64]
        ).astype(BF)


def merge_node(partials):
    return pl.pallas_call(
        merge_kernel,
        out_shape=jax.ShapeDtypeStruct((4, 80, 128), BF),
        in_specs=[whole((32, 48, 128))],
        out_specs=whole((4, 80, 128)),
        compiler_params=params(),
        name="merge_node",
    )(partials)


def local_kernel(
    info, leaf_ref, lengths_ref, kown, vown, p1, p2, p3, root_ref, l0, l1, l2, l3,
    out0, out1, out2, out3, gathered, outgoing,
):
    y = info[0]
    zl = info[1]
    for s, ref in enumerate((l0, l1, l2, l3)):
        gathered[(zl - s) & 3] = ref[...]
    leaf_row = jnp.broadcast_to(leaf_ref[...].astype(F32), (128, 128))
    leaf_col = leaf_row.T
    first_half = (y & 1) * 2
    suffix_k = jnp.concatenate(
        [gathered[first_half, 128:256], gathered[first_half + 1, 128:256]], axis=1
    )
    suffix_v = jnp.concatenate(
        [gathered[first_half, 256:384], gathered[first_half + 1, 256:384]], axis=1
    )
    root = root_ref[...].reshape(8, 4, 4, 32, 128)
    root_parts = [root[:, :, j].reshape(1024, 128) for j in range(4)]
    root_k = jnp.concatenate(root_parts[0:2], axis=1)
    root_v = jnp.concatenate(root_parts[2:4], axis=1)
    leaf_keys = [kown[...]] + [piece(ref, 0) for ref in (p1, p2, p3)]
    leaf_values = [vown[...]] + [piece(ref, 1) for ref in (p1, p2, p3)]
    token = iota((128, 128), 0)
    key_token = iota((128, 128), 1)
    suffix_ok = (leaf_row == leaf_col) & (key_token <= token) & ((key_token & 3) == zl)
    key_slot = iota((1, 512), 1)
    first = (iota((128, 128), 0) >> 4) * 16
    for h in range(2):
        queries = jnp.concatenate([gathered[2 * h, 0:128], gathered[2 * h + 1, 0:128]], axis=1)
        scores = [score(queries, root_k)]
        for s in range(4):
            source = (y - s) & 3
            place = (source * 4 + zl) * 16 + (key_slot & 15)
            key_leaf = jnp.where(place < lengths_ref[...], key_slot >> 4, -1).astype(F32)
            scores.append(
                jnp.where(leaf_col[:, 0:1] == key_leaf, score(queries, leaf_keys[s]), NEG)
            )
        scores.append(jnp.where(suffix_ok, score(queries, suffix_k), NEG))
        highest, total, summed = softmax_parts(scores, [root_v] + leaf_values + [suffix_v])
        stats = lane_stats(highest, total, first)
        packed = stats[0:16]
        for g in range(1, 8):
            packed = packed + stats[g * 16 : (g + 1) * 16]
        for half in range(2):
            outgoing[2 * h + half, 0:128] = summed[:, half * 128 : (half + 1) * 128].astype(BF)
            outgoing[2 * h + half, 128:144] = packed.astype(BF)
    for s, ref in enumerate((out0, out1, out2, out3)):
        ref[...] = outgoing[(zl + s) & 3]


def local_attend(info, leaf, lengths, cache, pieces, root, gathered):
    head = pl.BlockSpec((512, 256), lambda i, info: (0, info[0]))
    head_value = pl.BlockSpec((512, 256), lambda i, info: (0, 4 + info[0]))
    full = lambda shape: pl.BlockSpec(shape, lambda i, info: (0,) * len(shape))
    return pl.pallas_call(
        local_kernel,
        out_shape=tuple(jax.ShapeDtypeStruct((144, 128), BF) for _ in range(4)),
        grid_spec=pltpu.PrefetchScalarGridSpec(
            num_scalar_prefetch=1,
            grid=(1,),
            in_specs=[full((1, 128)), full((1, 512)), head, head_value]
            + [pl.BlockSpec((2048, 128), lambda i, info: (1, 0))] * 3
            + [full((8, 512, 128))]
            + [full((384, 128))] * 4,
            out_specs=tuple(full((144, 128)) for _ in range(4)),
            scratch_shapes=[pltpu.VMEM((4, 384, 128), BF), pltpu.VMEM((4, 144, 128), BF)],
        ),
        compiler_params=params(),
        cost_estimate=pl.CostEstimate(
            flops=LOCAL_FLOPS, transcendentals=1_000_000, bytes_accessed=8_000_000
        ),
        name="local_attend",
    )(info, leaf, lengths, cache, cache, *pieces, in_hbm(root), *gathered)


def final_kernel(slot_ref, branch_ref, l0, l1, l2, l3, out_ref):
    pick = jnp.where(iota((256, 128), 0) == slot_ref[...], 1.0, 0.0).astype(BF)

    def to_tokens(values):
        return lax.dot_general(
            pick, values, (((0,), (0,)), ((), ())), preferred_element_type=F32
        )

    branch = branch_ref[...]
    branch_sum = to_tokens(branch[:, 0:64].reshape(256, 128))
    lane16 = iota((16, 128), 1) >> 5
    spread = []
    for z in range(4):
        stat = branch[z, 64:80].astype(F32)
        for g in range(4):
            spread.append(jnp.where(lane16 == g, stat, 0.0))
    branch_stat = to_tokens(jnp.concatenate(spread, axis=0).astype(BF))
    lane = iota((128, 128), 1)

    def lane_pick(values, hit):
        return jnp.sum(jnp.where(hit, values, 0.0), axis=1, keepdims=True)

    column = lane & 31
    peaks = [lane_pick(branch_stat, column == 0)]
    totals = [lane_pick(branch_stat, (column == 1) | (column == 2))]
    sums = [branch_sum]
    first = (iota((128, 128), 0) >> 4) * 16
    for ref in (l0, l1, l2, l3):
        sums.append(ref[0:128].astype(F32))
        stat = ref[128:144].astype(F32)
        stat = jnp.concatenate([stat] * 8, axis=0)
        peaks.append(lane_pick(stat, lane == first))
        totals.append(lane_pick(stat, (lane == first + 1) | (lane == first + 2)))
    highest = peaks[0]
    for peak in peaks[1:]:
        highest = jnp.maximum(highest, peak)
    total = 0.0
    summed = 0.0
    for peak, part, value in zip(peaks, totals, sums):
        factor = jnp.exp(peak - highest)
        total = total + factor * part
        summed = summed + factor * value
    out_ref[...] = (summed / total).astype(BF)


def finish(slot, branch, parts):
    return pl.pallas_call(
        final_kernel,
        out_shape=jax.ShapeDtypeStruct((128, 128), BF),
        in_specs=[whole((1, 128)), whole((4, 80, 128))] + [whole((144, 128))] * 4,
        out_specs=whole((128, 128)),
        compiler_params=params(),
        name="finish",
    )(slot, branch, *parts)


def shift(values, axis, step):
    return lax.ppermute(values, axis, [(i, (i + step) % 4) for i in range(4)])


def exchange(values, axis):
    return lax.all_to_all(values, axis, split_axis=0, concat_axis=0, tiled=True)


def on_device(
    queries, suffix_cache, suffix_leaf, leaf_parent, root_cache,
    branch_cache, branch_length, leaf_cache, leaf_length,
):
    y = lax.axis_index("y")
    zl = lax.axis_index("zl")
    info = jnp.stack([y, zl, branch_length[0]]).astype(jnp.int32)
    branch_rows = branch_cache.reshape(512, 2048)
    leaf_rows = leaf_cache.reshape(512, 2048)

    tie = lax.optimization_barrier
    routed, slot, split = first_stage(
        leaf_parent, suffix_leaf, queries, root_cache, suffix_cache
    )
    own = exchange(split, "y")
    sent = pack_caches(info, branch_rows, leaf_rows)
    pieces = [shift(sent[s], "y", s + 1) for s in range(3)]
    onward = jnp.concatenate(
        [routed, jnp.broadcast_to(own[:, 0:32].reshape(1, 128, 128), (4, 128, 128))], axis=1
    )
    arrived = exchange(onward, "zh")
    def chosen(source):
        return lax.dynamic_index_in_dim(own, source, 0, keepdims=False)[32:160]

    mine = jnp.concatenate([queries, chosen(y >> 1), chosen(2 + (y >> 1))], axis=0)
    gathered = [mine] + [shift(mine, "zl", s + 1) for s in range(3)]
    arrived, lengths, gathered[1], gathered[2] = tie((arrived, key_lengths(leaf_length), gathered[1], gathered[2]))

    onward = arrived[:, 0:64].reshape(4, 8, 8, 128).transpose(1, 0, 2, 3).reshape(8, 1, 32, 128)
    onward = jnp.broadcast_to(onward, (8, 4, 32, 128)).reshape(32, 32, 128)
    root = arrived[:, 64:192].reshape(4, 4, 4, 8, 128).transpose(1, 2, 0, 3, 4)
    onward, root = tie((onward, root.reshape(512, 128)))
    root_all = lax.all_gather(root, XC, axis=0, tiled=False)
    node_queries = exchange(onward, XCZ)

    partials = branch_attend(arrive(info, pieces), node_queries, branch_rows, pieces)
    returned = exchange(partials, XCZ)
    merged = merge_node(returned)
    local = local_attend(info, suffix_leaf, lengths, leaf_rows, pieces, root_all, gathered)
    merged, own_part = tie((merged, local[0]))
    back = exchange(merged, "zh")
    parts = [own_part] + [shift(local[s + 1], "zl", s + 1) for s in range(3)]
    return finish(slot, back, parts)


def solution(mesh):
    fine = Mesh(mesh.devices.reshape(4, 4, 2, 4, 4), ("zh", "x", "core", "y", "zl"))
    in_specs = (
        P(ROW, COL),
        P(ROW, COL),
        P(ROW, None),
        P(ROW, None),
        P(ROW + COL, None),
        P(ROW, COL, None),
        P(ROW),
        P(ROW, COL, None),
        P(ROW),
    )
    return jax.shard_map(
        on_device, mesh=fine, in_specs=in_specs, out_specs=P(ROW, COL), check_vma=False
    )
```

```python
import jax
import jax.numpy as jnp
from jax import lax
from jax.experimental import pallas as pl
from jax.experimental.pallas import tpu as pltpu
from jax.sharding import Mesh, PartitionSpec as P

ROW = ("zh", "x", "core")
COL = ("y", "zl")
XC = ("x", "core")
XCZ = ("x", "core", "zl")
BF = jnp.bfloat16
F32 = jnp.float32
NEG = -1e30
FLOOR = -1e29
COST_FLOPS = 15_000_000_000
LOCAL_FLOPS = 12_000_000_000
LENGTH_FLOPS = 6_000_000_000
VMEM_LIMIT = 32 * 1024 * 1024


def iota(shape, dim):
    return lax.broadcasted_iota(jnp.int32, shape, dim)


def whole(shape):
    return pl.BlockSpec(shape, lambda: (0,) * len(shape))


SMEM = pl.BlockSpec(memory_space=pltpu.SMEM)
HBM = pl.BlockSpec(memory_space=pltpu.HBM)


def in_hbm(value):
    return pltpu.with_memory_space_constraint(value, pltpu.HBM)


def params():
    return pltpu.CompilerParams(vmem_limit_bytes=VMEM_LIMIT)


def first_kernel(
    parent, leaf_hbm, q_hbm, root_hbm, suffix_hbm, out_ref, slot_ref, split_ref,
    leaf_ref, q_ref, root_ref, suffix_ref, sems,
):
    copies = [
        pltpu.make_async_copy(source, target, sems.at[i])
        for i, (source, target) in enumerate(
            ((root_hbm, root_ref), (leaf_hbm, leaf_ref), (q_hbm, q_ref), (suffix_hbm, suffix_ref))
        )
    ]
    for copy in copies:
        copy.start()
    for copy in copies:
        copy.wait()
    root = root_ref[...].astype(F32)
    for target in range(4):
        lanes = [kv * 1024 + target * 256 + half * 128 for kv in range(2) for half in range(2)]
        split_ref[target, 32:160] = suffix_ref[...]
        split_ref[target, 0:32] = jnp.concatenate([root[:, l : l + 128] for l in lanes], axis=0).astype(BF)
    leaf = leaf_ref[...]
    across = jnp.broadcast_to(leaf.astype(F32), (128, 128))
    down = across.T
    before = iota((128, 128), 0) < iota((128, 128), 1)
    rank = jnp.sum(jnp.where((across == down) & before, 1.0, 0.0), axis=0, keepdims=True)
    node = jnp.zeros((1, 128), jnp.int32)
    for leaf_id in range(32):
        node = jnp.where(leaf == leaf_id, parent[0, leaf_id], node)
    slot = node * 8 + rank.astype(jnp.int32)
    slot_ref[...] = slot
    pick = jnp.where(iota((256, 128), 0) == slot, 1.0, 0.0).astype(BF)
    routed = jnp.dot(pick, q_ref[...], preferred_element_type=F32).astype(BF)
    out_ref[...] = routed.reshape(4, 64, 128)


def first_stage(parent, leaf, queries, root, suffix):
    return pl.pallas_call(
        first_kernel,
        out_shape=(
            jax.ShapeDtypeStruct((4, 64, 128), BF),
            jax.ShapeDtypeStruct((1, 128), jnp.int32),
            jax.ShapeDtypeStruct((4, 160, 128), BF),
        ),
        in_specs=[SMEM, HBM, HBM, HBM, HBM],
        out_specs=(whole((4, 64, 128)), whole((1, 128)), whole((4, 160, 128))),
        scratch_shapes=[
            pltpu.VMEM((1, 128), jnp.int32),
            pltpu.VMEM((128, 128), BF),
            pltpu.VMEM((8, 2048), BF),
            pltpu.VMEM((128, 128), BF),
            pltpu.SemaphoreType.DMA((4,)),
        ],
        compiler_params=params(),
        name="first_stage",
    )(parent, in_hbm(leaf), in_hbm(queries), in_hbm(root), in_hbm(suffix))


def pack_kernel(info, branch, leaf, sent1, sent2, sent3, branch_buf, leaf_buf, loads, stores):
    pairs = ((branch, branch_buf), (leaf, leaf_buf))
    fetches = [
        pltpu.make_async_copy(cache, buf, loads.at[i]) for i, (cache, buf) in enumerate(pairs)
    ]
    for fetch in fetches:
        fetch.start()
    moves = []
    for i, (_, buf) in enumerate(pairs):
        fetches[i].wait()
        for s, sent in enumerate((sent1, sent2, sent3)):
            target = (info[0] + (s + 1)) & 3
            for part in range(4):
                start = (part // 2) * 1024 + (part % 2) * 128
                lane = pl.multiple_of(target * 256 + start, 128)
                moves.append(
                    pltpu.make_async_copy(
                        buf.at[:, pl.ds(lane, 128)],
                        sent.at[pl.ds(i * 2048 + part * 512, 512), :],
                        stores.at[i, s, part],
                    )
                )
                moves[-1].start()
    for move in moves:
        move.wait()


def pack_caches(info, branch, leaf):
    return pl.pallas_call(
        pack_kernel,
        out_shape=tuple(jax.ShapeDtypeStruct((4096, 128), BF) for _ in range(3)),
        in_specs=[SMEM, HBM, HBM],
        out_specs=(HBM, HBM, HBM),
        scratch_shapes=[
            pltpu.VMEM((512, 2048), BF),
            pltpu.VMEM((512, 2048), BF),
            pltpu.SemaphoreType.DMA((2,)),
            pltpu.SemaphoreType.DMA((2, 3, 4)),
        ],
        compiler_params=params(),
        name="pack_caches",
    )(info, in_hbm(branch), in_hbm(leaf))


def lengths_kernel(lengths, out):
    leaf = iota((1, 512), 1) >> 4
    row = jnp.zeros((1, 512), jnp.int32)
    for i in range(32):
        row = jnp.where(leaf == i, lengths[i], row)
    out[...] = row


def key_lengths(lengths):
    return pl.pallas_call(
        lengths_kernel,
        out_shape=jax.ShapeDtypeStruct((1, 512), jnp.int32),
        in_specs=[SMEM],
        out_specs=whole((1, 512)),
        compiler_params=params(),
        cost_estimate=pl.CostEstimate(
            flops=LENGTH_FLOPS, transcendentals=1_000_000, bytes_accessed=8_000_000
        ),
        name="key_lengths",
    )(lengths)


def arrive_kernel(info, p1, p2, p3, out):
    for i in range(3):
        out[i] = info[i]


def arrive(info, pieces):
    return pl.pallas_call(
        arrive_kernel,
        out_shape=jax.ShapeDtypeStruct((3,), jnp.int32),
        in_specs=[SMEM, HBM, HBM, HBM],
        out_specs=SMEM,
        compiler_params=params(),
        cost_estimate=pl.CostEstimate(
            flops=COST_FLOPS, transcendentals=1_000_000, bytes_accessed=8_000_000
        ),
        name="arrive",
    )(info, *pieces)


def softmax_parts(scores, values):
    highest = scores[0].max(axis=1, keepdims=True)
    for part in scores[1:]:
        highest = jnp.maximum(highest, part.max(axis=1, keepdims=True))
    highest = jnp.maximum(highest, FLOOR).astype(BF).astype(F32)
    total = 0.0
    summed = 0.0
    for part, value in zip(scores, values):
        weights = jnp.exp(part - highest)
        total = total + jnp.sum(weights, axis=1, keepdims=True)
        summed = summed + jnp.dot(weights.astype(BF), value, preferred_element_type=F32)
    return highest, total, summed


def score(queries, keys):
    return lax.dot_general(
        queries, keys, (((1,), (1,)), ((), ())), preferred_element_type=F32
    ) * (1.0 / 16.0)


def split_total(total):
    upper = total.astype(BF).astype(F32)
    return upper, total - upper


def lane_stats(highest, total, first):
    upper, lower = split_total(total)
    rows = highest.shape[0]
    lane = iota((rows, 128), 1)
    place = jnp.where(lane == first, highest, 0.0)
    place = jnp.where(lane == first + 1, upper, place)
    return jnp.where(lane == first + 2, lower, place)


def piece(ref, kv):
    base = kv * 1024
    return jnp.concatenate([ref[base : base + 512], ref[base + 512 : base + 1024]], axis=1)


def branch_kernel(info, q_ref, kown, vown, p1, p2, p3, out_ref):
    y = info[0]
    zl = info[1]
    length = info[2]
    loaded = q_ref[...].reshape(8, 4, 32, 128)
    blocks = [loaded[:, z].reshape(256, 128) for z in range(4)]
    keys = [kown[...]] + [piece(ref, 0) for ref in (p1, p2, p3)]
    values = [vown[...]] + [piece(ref, 1) for ref in (p1, p2, p3)]
    row16 = iota((256, 128), 0) & 31
    for h in range(2):
        queries = jnp.concatenate([blocks[2 * h], blocks[2 * h + 1]], axis=1)
        scores = []
        for s in range(4):
            place = (((y - s) & 3) * 4 + zl) * 512 + iota((256, 512), 1)
            scores.append(jnp.where(place < length, score(queries, keys[s]), NEG))
        highest, total, summed = softmax_parts(scores, values)
        first = jnp.where(row16 < 16, 0, 64)
        stats = lane_stats(highest, total, first)
        for xc in range(8):
            low = xc * 32
            packed = (stats[low : low + 16] + stats[low + 16 : low + 32]).astype(BF)
            for half in range(2):
                out_ref[xc * 4 + 2 * h + half, 0:32] = summed[
                    low : low + 32, half * 128 : (half + 1) * 128
                ].astype(BF)
                out_ref[xc * 4 + 2 * h + half, 32:48] = packed


def branch_attend(info, arrived, cache, pieces):
    head = pl.BlockSpec((512, 256), lambda i, info: (0, info[0]))
    head_value = pl.BlockSpec((512, 256), lambda i, info: (0, 4 + info[0]))
    full = lambda shape: pl.BlockSpec(shape, lambda i, info: (0,) * len(shape))
    return pl.pallas_call(
        branch_kernel,
        out_shape=jax.ShapeDtypeStruct((32, 48, 128), BF),
        grid_spec=pltpu.PrefetchScalarGridSpec(
            num_scalar_prefetch=1,
            grid=(1,),
            in_specs=[full((32, 32, 128)), head, head_value] + [pl.BlockSpec((2048, 128), lambda i, info: (0, 0))] * 3,
            out_specs=full((32, 48, 128)),
        ),
        compiler_params=params(),
        name="branch_attend",
    )(info, arrived, cache, cache, *pieces)


def merge_kernel(in_ref, out_ref):
    loaded = in_ref[...].astype(F32).reshape(8, 4, 48, 128)
    data = [loaded[:, z, 0:32] for z in range(4)]
    stats = [loaded[:, z, 32:48] for z in range(4)]

    def column(stat, j):
        return jnp.concatenate([stat[:, :, j : j + 1], stat[:, :, 64 + j : 65 + j]], axis=1)

    peaks = [column(stat, 0) for stat in stats]
    highest = jnp.maximum(jnp.maximum(peaks[0], peaks[1]), jnp.maximum(peaks[2], peaks[3]))
    total = 0.0
    summed = 0.0
    for z in range(4):
        factor = jnp.exp(peaks[z] - highest)
        total = total + factor * (column(stats[z], 1) + column(stats[z], 2))
        summed = summed + factor * data[z]
    highest = highest.reshape(8, 4, 8, 1)
    total = total.reshape(8, 4, 8, 1)
    summed = summed.reshape(8, 4, 8, 128)
    first = (iota((64, 128), 0) >> 4) * 32
    for z in range(4):
        out_ref[z, 0:64] = summed[:, z].reshape(64, 128).astype(BF)
        placed = lane_stats(highest[:, z].reshape(64, 1), total[:, z].reshape(64, 1), first)
        out_ref[z, 64:80] = (
            placed[0:16] + placed[16:32] + placed[32:48] + placed[48:64]
        ).astype(BF)


def merge_node(partials):
    return pl.pallas_call(
        merge_kernel,
        out_shape=jax.ShapeDtypeStruct((4, 80, 128), BF),
        in_specs=[whole((32, 48, 128))],
        out_specs=whole((4, 80, 128)),
        compiler_params=params(),
        name="merge_node",
    )(partials)


def local_kernel(
    info, leaf_ref, lengths_ref, kown, vown, p1, p2, p3, root_ref, l0, l1, l2, l3,
    out0, out1, out2, out3, gathered, outgoing,
):
    y = info[0]
    zl = info[1]
    for s, ref in enumerate((l0, l1, l2, l3)):
        gathered[(zl - s) & 3] = ref[...]
    leaf_row = jnp.broadcast_to(leaf_ref[...].astype(F32), (128, 128))
    leaf_col = leaf_row.T
    first_half = (y & 1) * 2
    suffix_k = jnp.concatenate(
        [gathered[first_half, 128:256], gathered[first_half + 1, 128:256]], axis=1
    )
    suffix_v = jnp.concatenate(
        [gathered[first_half, 256:384], gathered[first_half + 1, 256:384]], axis=1
    )
    root = root_ref[...].reshape(8, 4, 4, 32, 128)
    root_parts = [root[:, :, j].reshape(1024, 128) for j in range(4)]
    root_k = jnp.concatenate(root_parts[0:2], axis=1)
    root_v = jnp.concatenate(root_parts[2:4], axis=1)
    leaf_keys = [kown[...]] + [piece(ref, 0) for ref in (p1, p2, p3)]
    leaf_values = [vown[...]] + [piece(ref, 1) for ref in (p1, p2, p3)]
    token = iota((128, 128), 0)
    key_token = iota((128, 128), 1)
    suffix_ok = (leaf_row == leaf_col) & (key_token <= token) & ((key_token & 3) == zl)
    key_slot = iota((1, 512), 1)
    first = (iota((128, 128), 0) >> 4) * 16
    for h in range(2):
        queries = jnp.concatenate([gathered[2 * h, 0:128], gathered[2 * h + 1, 0:128]], axis=1)
        scores = [score(queries, root_k)]
        for s in range(4):
            source = (y - s) & 3
            place = (source * 4 + zl) * 16 + (key_slot & 15)
            key_leaf = jnp.where(place < lengths_ref[...], key_slot >> 4, -1).astype(F32)
            scores.append(
                jnp.where(leaf_col[:, 0:1] == key_leaf, score(queries, leaf_keys[s]), NEG)
            )
        scores.append(jnp.where(suffix_ok, score(queries, suffix_k), NEG))
        highest, total, summed = softmax_parts(scores, [root_v] + leaf_values + [suffix_v])
        stats = lane_stats(highest, total, first)
        packed = stats[0:16]
        for g in range(1, 8):
            packed = packed + stats[g * 16 : (g + 1) * 16]
        for half in range(2):
            outgoing[2 * h + half, 0:128] = summed[:, half * 128 : (half + 1) * 128].astype(BF)
            outgoing[2 * h + half, 128:144] = packed.astype(BF)
    for s, ref in enumerate((out0, out1, out2, out3)):
        ref[...] = outgoing[(zl + s) & 3]


def local_attend(info, leaf, lengths, cache, pieces, root, gathered):
    head = pl.BlockSpec((512, 256), lambda i, info: (0, info[0]))
    head_value = pl.BlockSpec((512, 256), lambda i, info: (0, 4 + info[0]))
    full = lambda shape: pl.BlockSpec(shape, lambda i, info: (0,) * len(shape))
    return pl.pallas_call(
        local_kernel,
        out_shape=tuple(jax.ShapeDtypeStruct((144, 128), BF) for _ in range(4)),
        grid_spec=pltpu.PrefetchScalarGridSpec(
            num_scalar_prefetch=1,
            grid=(1,),
            in_specs=[full((1, 128)), full((1, 512)), head, head_value]
            + [pl.BlockSpec((2048, 128), lambda i, info: (1, 0))] * 3
            + [full((8, 512, 128))]
            + [full((384, 128))] * 4,
            out_specs=tuple(full((144, 128)) for _ in range(4)),
            scratch_shapes=[pltpu.VMEM((4, 384, 128), BF), pltpu.VMEM((4, 144, 128), BF)],
        ),
        compiler_params=params(),
        cost_estimate=pl.CostEstimate(
            flops=LOCAL_FLOPS, transcendentals=1_000_000, bytes_accessed=8_000_000
        ),
        name="local_attend",
    )(info, leaf, lengths, cache, cache, *pieces, in_hbm(root), *gathered)


def final_kernel(slot_ref, branch_ref, l0, l1, l2, l3, out_ref):
    pick = jnp.where(iota((256, 128), 0) == slot_ref[...], 1.0, 0.0).astype(BF)

    def to_tokens(values):
        return lax.dot_general(
            pick, values, (((0,), (0,)), ((), ())), preferred_element_type=F32
        )

    branch = branch_ref[...]
    branch_sum = to_tokens(branch[:, 0:64].reshape(256, 128))
    lane16 = iota((16, 128), 1) >> 5
    spread = []
    for z in range(4):
        stat = branch[z, 64:80].astype(F32)
        for g in range(4):
            spread.append(jnp.where(lane16 == g, stat, 0.0))
    branch_stat = to_tokens(jnp.concatenate(spread, axis=0).astype(BF))
    lane = iota((128, 128), 1)

    def lane_pick(values, hit):
        return jnp.sum(jnp.where(hit, values, 0.0), axis=1, keepdims=True)

    column = lane & 31
    peaks = [lane_pick(branch_stat, column == 0)]
    totals = [lane_pick(branch_stat, (column == 1) | (column == 2))]
    sums = [branch_sum]
    first = (iota((128, 128), 0) >> 4) * 16
    for ref in (l0, l1, l2, l3):
        sums.append(ref[0:128].astype(F32))
        stat = ref[128:144].astype(F32)
        stat = jnp.concatenate([stat] * 8, axis=0)
        peaks.append(lane_pick(stat, lane == first))
        totals.append(lane_pick(stat, (lane == first + 1) | (lane == first + 2)))
    highest = peaks[0]
    for peak in peaks[1:]:
        highest = jnp.maximum(highest, peak)
    total = 0.0
    summed = 0.0
    for peak, part, value in zip(peaks, totals, sums):
        factor = jnp.exp(peak - highest)
        total = total + factor * part
        summed = summed + factor * value
    out_ref[...] = (summed / total).astype(BF)


def finish(slot, branch, parts):
    return pl.pallas_call(
        final_kernel,
        out_shape=jax.ShapeDtypeStruct((128, 128), BF),
        in_specs=[whole((1, 128)), whole((4, 80, 128))] + [whole((144, 128))] * 4,
        out_specs=whole((128, 128)),
        compiler_params=params(),
        name="finish",
    )(slot, branch, *parts)


def shift(values, axis, step):
    return lax.ppermute(values, axis, [(i, (i + step) % 4) for i in range(4)])


def exchange(values, axis):
    return lax.all_to_all(values, axis, split_axis=0, concat_axis=0, tiled=True)


def on_device(
    queries, suffix_cache, suffix_leaf, leaf_parent, root_cache,
    branch_cache, branch_length, leaf_cache, leaf_length,
):
    y = lax.axis_index("y")
    zl = lax.axis_index("zl")
    info = jnp.stack([y, zl, branch_length[0]]).astype(jnp.int32)
    branch_rows = branch_cache.reshape(512, 2048)
    leaf_rows = leaf_cache.reshape(512, 2048)

    tie = lax.optimization_barrier
    routed, slot, split = first_stage(
        leaf_parent, suffix_leaf, queries, root_cache, suffix_cache
    )
    own = exchange(split, "y")
    sent = pack_caches(info, branch_rows, leaf_rows)
    pieces = [shift(sent[s], "y", s + 1) for s in range(3)]
    onward = jnp.concatenate(
        [routed, jnp.broadcast_to(own[:, 0:32].reshape(1, 128, 128), (4, 128, 128))], axis=1
    )
    arrived = exchange(onward, "zh")
    def chosen(source):
        return lax.dynamic_index_in_dim(own, source, 0, keepdims=False)[32:160]

    mine = jnp.concatenate([queries, chosen(y >> 1), chosen(2 + (y >> 1))], axis=0)
    gathered = [mine] + [shift(mine, "zl", s + 1) for s in range(2)]
    arrived, lengths, gathered[1], gathered[2] = tie((arrived, key_lengths(leaf_length), gathered[1], gathered[2]))

    onward = arrived[:, 0:64].reshape(4, 8, 8, 128).transpose(1, 0, 2, 3).reshape(8, 1, 32, 128)
    onward = jnp.broadcast_to(onward, (8, 4, 32, 128)).reshape(32, 32, 128)
    root = arrived[:, 64:192].reshape(4, 4, 4, 8, 128).transpose(1, 2, 0, 3, 4)
    onward, root = tie((onward, root.reshape(512, 128)))
    root_all = lax.all_gather(root, XC, axis=0, tiled=False)
    node_queries = exchange(onward, XCZ)
    node_queries, last = tie((node_queries, mine))
    gathered.append(shift(last, "zl", 3))

    partials = branch_attend(arrive(info, pieces), node_queries, branch_rows, pieces)
    returned = exchange(partials, XCZ)
    merged = merge_node(returned)
    local = local_attend(info, suffix_leaf, lengths, leaf_rows, pieces, root_all, gathered)
    merged, own_part = tie((merged, local[0]))
    back = exchange(merged, "zh")
    parts = [own_part] + [shift(local[s + 1], "zl", s + 1) for s in range(3)]
    return finish(slot, back, parts)


def solution(mesh):
    fine = Mesh(mesh.devices.reshape(4, 4, 2, 4, 4), ("zh", "x", "core", "y", "zl"))
    in_specs = (
        P(ROW, COL),
        P(ROW, COL),
        P(ROW, None),
        P(ROW, None),
        P(ROW + COL, None),
        P(ROW, COL, None),
        P(ROW),
        P(ROW, COL, None),
        P(ROW),
    )
    return jax.shard_map(
        on_device, mesh=fine, in_specs=in_specs, out_specs=P(ROW, COL), check_vma=False
    )
```
